512 devices in a mesh: ctx: 32 (over x, z_lo, core), tp: 16 (over y, z_hi).
Axes of the slice: x: 4, y: 4, z: 16 (z_hi: 4, z_lo: 4; z = z_hi * 4 + z_lo), core: 2. Of those that a mesh axis runs over, the one named last changes fastest.
Arguments:
- attention_out: bfloat16 [512, 8192], P('ctx', 'tp'), may hold values from -6 to 6
- w_out: bfloat16 [8192, 8192], P('tp', 'ctx'), may hold values from -0.0625 to 0.0625
- residual: bfloat16 [512, 8192], P(('ctx', 'tp')), may hold values from -6 to 6
- norm_gain: float32 [8192], replicated, may hold values from 0.1 to 1.9
- w_gate: bfloat16 [28672, 8192], P(('ctx', 'tp')), may hold values from -0.0625 to 0.0625
- w_up: bfloat16 [28672, 8192], P(('ctx', 'tp')), may hold values from -0.0625 to 0.0625
- w_down: bfloat16 [32, 896, 8192], P(None, 'tp', 'ctx'), may hold values from -0.03125 to 0.03125
Outputs:
- mixed: bfloat16 [512, 8192], P(('ctx', 'tp'))
The draws below stay inside these ranges and needn't reach their ends.
All inputs are finite; a program needn't handle non-finite values.
Results may differ from the reference program's by a relative error of at most 0.02.
Values may be sent and summed in bfloat16 or wider, within the bound.
No kernel may reach another device: no remote copies, remote signals or barrier semaphores. Data moves between devices by JAX's collectives and lax.ppermute only.
A program may use at most 64 MiB of HBM per device.

```python
import jax
import jax.numpy as jnp
from jax import lax

D = 8192
FF = 28672
TOKENS = 512
HD = 8192
N_CTX = 32


def level_of(key, dims, shards, smallest, high):
    loudness, own = 1.0, jax.random.fold_in(key, 6)
    for axis_at, blocks in shards:
        heights = jnp.exp(jax.random.uniform(jax.random.fold_in(own, axis_at), (blocks,), jnp.float32, smallest / len(shards), high / len(shards)))
        loudness = loudness * jnp.repeat(heights, dims[axis_at] // blocks).reshape([-1 if axis == axis_at else 1 for axis in range(len(dims))])
    return loudness


def gaussian(stream_key, shape, deviation, bound, pieces=(), dtype=jnp.bfloat16):
    array = jax.random.normal(stream_key, shape, jnp.float32) * deviation
    if len(pieces) > 0:
        array = level_of(stream_key, shape, pieces, -0.22, 0.18) * array
    return jnp.clip(array, min=-bound, max=bound).astype(dtype)


def setup_inputs(seed: int = 0) -> dict:
    seeds = jax.random.split(jax.random.key(seed), 8)
    attention_out = gaussian(seeds[0], (TOKENS, HD), 1.0, 6.0, ((0, 32), (1, 16)))
    w_out = gaussian(seeds[1], (HD, D), HD ** -0.5, 0.0625, ((0, 16), (1, 32)))
    residual = gaussian(seeds[2], (TOKENS, D), 1.0, 6.0, ((0, 512),))
    norm_gain = jnp.clip(1.0 + 0.18 * jax.random.normal(seeds[3], (D,), jnp.float32), 0.1, 1.9)
    w_gate = gaussian(seeds[4], (FF, D), D ** -0.5, 0.0625, ((0, 512),))
    w_up = gaussian(seeds[5], (FF, D), D ** -0.5, 0.0625, ((0, 512),))
    w_down = gaussian(seeds[6], (N_CTX, FF // N_CTX, D), FF ** -0.5, 0.03125, ((1, 16), (2, 32)))
    return {"attention_out": attention_out, "w_out": w_out, "residual": residual, "norm_gain": norm_gain, "w_gate": w_gate, "w_up": w_up, "w_down": w_down}


def reference(attention_out, w_out, residual, norm_gain, w_gate, w_up, w_down):
    proj = jnp.dot(attention_out, w_out, preferred_element_type=jnp.float32)
    carried = residual.astype(jnp.float32) + proj
    mean_square = lax.optimization_barrier(jnp.mean(carried * carried, axis=-1, keepdims=True))
    normed = (carried * lax.rsqrt(mean_square + 1e-05) * norm_gain).astype(jnp.bfloat16)
    gate = jnp.dot(normed, w_gate.T, preferred_element_type=jnp.float32)
    up_part = jnp.dot(normed, w_up.T, preferred_element_type=jnp.float32)
    hidden = (jax.nn.silu(gate) * up_part).astype(jnp.bfloat16)
    down_matrix = w_down.reshape(FF, D)
    down = jnp.dot(hidden, down_matrix, preferred_element_type=jnp.float32)
    return (carried + down).astype(jnp.bfloat16)
```

```python
import jax
import jax.numpy as jnp
from jax import lax
from jax.sharding import Mesh, PartitionSpec as P

F32 = jnp.float32
BF16 = jnp.bfloat16
EPS = 1e-05
X, ZL, Y, ZH = 4, 4, 4, 4
CORES = 2


def exchange(value, axes):
    return lax.all_to_all(value, axes, 0, 0, tiled=True)


def replicate(value, count):
    return lax.optimization_barrier(jnp.broadcast_to(value[None], (count,) + value.shape))


def split_two(value):
    high = value.astype(BF16)
    low = (value - high.astype(F32)).astype(BF16)
    return high, low


def shards(attention_out, w_out, residual, norm_gain, w_gate, w_up, w_down):
    x_at = lax.axis_index("x")
    zl_at = lax.axis_index("zl")
    core_at = lax.axis_index("core")
    y_at = lax.axis_index("y")
    zh_at = lax.axis_index("zh")
    d = residual.shape[1]
    t_rows, heads = attention_out.shape
    cols = w_out.shape[1]
    units = w_gate.shape[0]
    tokens = t_rows * X * ZL * CORES
    chunk = tokens // Y
    ctx_at = (x_at * ZL + zl_at) * CORES + core_at

    def weight_piece(at):
        def take(w):
            return lax.dynamic_index_in_dim(
                w.reshape(units, X, ZL, CORES * cols), at, 2, keepdims=False
            )
        return jnp.concatenate([take(w_gate), take(w_up)], axis=0)

    pieces = [weight_piece(zl_at)]
    for shift in range(1, ZL):
        piece = weight_piece((zl_at + shift) % ZL)
        pieces.append(
            lax.ppermute(piece, "zl", [(i, (i + shift) % ZL) for i in range(ZL)])
        )

    rows = 24
    sent = jnp.concatenate(
        [
            jnp.broadcast_to(attention_out[None], (X * ZL, t_rows, heads)),
            residual.reshape(X * ZL, 1, CORES * cols),
            jnp.zeros((X * ZL, rows - t_rows - 1, heads), BF16),
        ],
        axis=1,
    )
    gathered = exchange(sent, ("x", "zl"))
    gathered = lax.all_gather(gathered, "core", axis=0, tiled=False)
    att = gathered[:, :, :t_rows].reshape(tokens, heads)
    res_pair = gathered[:, :, t_rows].reshape(CORES * X * ZL, CORES, cols)
    res = lax.dynamic_index_in_dim(res_pair, core_at, 1, keepdims=False)

    partial = jnp.dot(att, w_out, preferred_element_type=F32)
    own_t = lax.broadcasted_iota(jnp.int32, (1, t_rows, 1), 1) == y_at * ZH + zh_at
    partial = partial.reshape(CORES * X * ZL, t_rows, cols) + jnp.where(
        own_t, res.astype(F32)[:, None, :], 0.0
    )
    by_y = exchange(partial.astype(BF16).reshape(Y, chunk, cols), "y")
    over_y = jnp.sum(by_y.astype(F32), axis=0).astype(BF16)
    by_zh = exchange(replicate(over_y, ZH), "zh")
    carried = jnp.sum(by_zh.astype(F32), axis=0)

    gain = lax.dynamic_slice_in_dim(norm_gain, ctx_at * cols, cols, 0)
    scaled = (carried * gain[None, :]).astype(BF16)
    square = jnp.sum(carried * carried, axis=1)
    high, low = split_two(square)
    extra = 16
    to_send = jnp.concatenate(
        [
            scaled,
            jnp.concatenate([high, low])[None, :],
            jnp.zeros((extra - 1, cols), BF16),
        ],
        axis=0,
    )
    spread = exchange(replicate(to_send, X * Y), ("x", "y"))
    spread = lax.all_gather(spread, "core", axis=0, tiled=False)
    spread = spread.reshape(CORES, X, Y, chunk + extra, cols)
    values = spread[:, :, :, :chunk]
    squares = spread[:, :, :, chunk].astype(F32).reshape(CORES, X, Y, 2, chunk)
    square_sum = jnp.sum(squares, axis=(0, 1, 3)).reshape(tokens)
    s_high, s_low = split_two(square_sum)

    lhs = jnp.transpose(values, (2, 3, 1, 0, 4)).reshape(tokens, X * CORES * cols)
    pad = 16
    totals = None
    outs = []
    for shift in range(ZL):
        weight = pieces[shift].reshape(2 * units, X * CORES * cols)
        part = lax.dot_general(
            weight, lhs, (((1,), (1,)), ((), ())), preferred_element_type=F32
        ).astype(BF16)
        outs.append(
            jnp.concatenate(
                [part, s_high[None], s_low[None], jnp.zeros((pad - 2, tokens), BF16)], axis=0
            )
        )
    total = outs[0].astype(F32)
    for shift in range(1, ZL):
        got = lax.ppermute(
            outs[shift], "zl", [(i, (i - shift) % ZL) for i in range(ZL)]
        )
        total = total + got.astype(F32)
    mean_square = (total[2 * units] + total[2 * units + 1]) * (1.0 / d)
    scale = lax.rsqrt(mean_square + EPS)[None, :]
    gate = total[:units] * scale
    up = total[units : 2 * units] * scale
    hidden = (jax.nn.silu(gate) * up).astype(BF16)

    hidden = exchange(replicate(hidden, ZL), "zl")
    hidden = exchange(replicate(hidden, X), "x")
    hidden = hidden.reshape(X * ZL, units, tokens)
    hidden = lax.all_gather(hidden, "core", axis=0, tiled=False)
    down_w = w_down.reshape(X * ZL, CORES, units, cols)
    down = None
    for core in range(CORES):
        term = lax.dot_general(
            hidden[core].reshape(X * ZL * units, tokens),
            down_w[:, core].reshape(X * ZL * units, cols),
            (((0,), (0,)), ((), ())),
            preferred_element_type=F32,
        )
        down = term if down is None else down + term
    holds = (lax.broadcasted_iota(jnp.int32, (Y, 1, 1), 0) == y_at) & (zh_at == 0)
    down = down.reshape(Y, chunk, cols) + jnp.where(holds, carried[None], 0.0)
    final = exchange(
        down.astype(BF16).reshape(tokens, cols // 128, 128), ("core", "x", "zl", "y", "zh")
    )
    final = final.reshape(CORES, X * ZL, Y * ZH, cols).astype(F32)
    mixed = jnp.sum(final, axis=2)
    mixed = jnp.transpose(mixed, (1, 0, 2)).reshape(1, d)
    return mixed.astype(BF16)


def solution(mesh):
    view = Mesh(
        mesh.devices.reshape(X, ZL, CORES, Y, ZH), ("x", "zl", "core", "y", "zh")
    )
    ctx = ("x", "zl", "core")
    tp = ("y", "zh")
    in_specs = (
        P(ctx, tp),
        P(tp, ctx),
        P(ctx + tp, None),
        P(),
        P(ctx + tp, None),
        P(ctx + tp, None),
        P(None, tp, ctx),
    )
    return jax.shard_map(
        shards, mesh=view, in_specs=in_specs, out_specs=P(ctx + tp, None), check_vma=False
    )
```

```python
import jax
import jax.numpy as jnp
from jax import lax
from jax.experimental import pallas as pl
from jax.experimental.pallas import tpu as pltpu
from jax.sharding import Mesh, PartitionSpec as P

F32 = jnp.float32
BF16 = jnp.bfloat16
EPS = 1e-05
X, ZL, Y, ZH = 4, 4, 4, 4
CORES = 2
EXTRA = 16


def exchange(value, axes):
    return lax.all_to_all(value, axes, 0, 0, tiled=True)


def replicate(value, count):
    return lax.optimization_barrier(jnp.broadcast_to(value[None], (count,) + value.shape))


def swap_cores(value):
    return lax.ppermute(value, "core", [(0, 1), (1, 0)])


def shift_y(value, shift):
    return lax.ppermute(value, "y", [(i, (i + shift) % Y) for i in range(Y)])


def vmem():
    return pl.BlockSpec(memory_space=pltpu.VMEM)


def smem():
    return pl.BlockSpec(memory_space=pltpu.SMEM)


def pack_rows(attention_out, residual):
    t_rows, heads = attention_out.shape
    wide = residual.shape[1] // (X * ZL)
    rows = 24

    def kernel(att_ref, res_ref, sent_ref):
        for to in range(X * ZL):
            sent_ref[to, :t_rows, :] = att_ref[...]
            sent_ref[to, t_rows:, :] = jnp.zeros((rows - t_rows, heads), BF16)
            sent_ref[to, t_rows : t_rows + 1, :] = res_ref[:, to * wide : (to + 1) * wide]

    return pl.pallas_call(
        kernel,
        out_shape=jax.ShapeDtypeStruct((X * ZL, rows, heads), BF16),
        in_specs=[vmem(), vmem()],
        out_specs=vmem(),
        compiler_params=pltpu.CompilerParams(vmem_limit_bytes=4 * 1024 * 1024),
        name="pack_rows",
    )(attention_out, residual)


def cut_weights(w_gate, w_up, norm_gain, y_at):
    units, d = w_gate.shape
    blocks = X * ZL
    wide = d // blocks
    part = wide // Y

    def kernel(at_ref, gate_ref, up_ref, gain_ref, *piece_refs):
        for shift in range(Y):
            to = lax.rem(at_ref[0] + shift, Y)
            for block in range(blocks):
                place = pl.ds(pl.multiple_of(block * wide + to * part, part), part)
                gain = gain_ref[:, place]
                both = jnp.concatenate(
                    [gate_ref[:, place].astype(F32) * gain, up_ref[:, place].astype(F32) * gain],
                    axis=0,
                )
                piece_refs[shift][:, block * part : (block + 1) * part] = both.astype(BF16)

    return pl.pallas_call(
        kernel,
        out_shape=[jax.ShapeDtypeStruct((2 * units, blocks * part), BF16)] * Y,
        in_specs=[smem(), vmem(), vmem(), vmem()],
        out_specs=[vmem()] * Y,
        compiler_params=pltpu.CompilerParams(vmem_limit_bytes=12 * 1024 * 1024),
        name="cut_weights",
    )(y_at.reshape(1), w_gate, w_up, norm_gain.reshape(1, d))


def sum_and_replicate(parts, count):
    pieces, rows, width = parts.shape

    def kernel(parts_ref, out_ref):
        total = parts_ref[0].astype(F32)
        for piece in range(1, pieces):
            total = total + parts_ref[piece].astype(F32)
        for to in range(count):
            out_ref[to] = total.astype(BF16)

    return pl.pallas_call(
        kernel,
        out_shape=jax.ShapeDtypeStruct((count, rows, width), BF16),
        in_specs=[vmem()],
        out_specs=vmem(),
        compiler_params=pltpu.CompilerParams(vmem_limit_bytes=4 * 1024 * 1024),
        name="sum_and_replicate",
    )(parts)


def carried_and_squares(parts, count):
    pieces, rows, width = parts.shape

    def kernel(parts_ref, out_ref):
        total = parts_ref[0].astype(F32)
        for piece in range(1, pieces):
            total = total + parts_ref[piece].astype(F32)
        square = jnp.sum(total * total, axis=0, keepdims=True)
        high = square.astype(BF16).astype(F32)
        tail = jnp.concatenate(
            [high, square - high, jnp.zeros((EXTRA - 2, width), F32)], axis=0
        ).astype(BF16)
        for to in range(count):
            out_ref[to, :rows, :] = total.astype(BF16)
            out_ref[to, rows:, :] = tail

    return pl.pallas_call(
        kernel,
        out_shape=jax.ShapeDtypeStruct((count, rows + EXTRA, width), BF16),
        in_specs=[vmem()],
        out_specs=vmem(),
        compiler_params=pltpu.CompilerParams(vmem_limit_bytes=4 * 1024 * 1024),
        name="carried_and_squares",
    )(parts)


def activate(parts, d, count):
    pieces, rows, tokens = parts.shape
    units = (rows - EXTRA) // 2

    def kernel(parts_ref, out_ref):
        total = parts_ref[0].astype(F32)
        for piece in range(1, pieces):
            total = total + parts_ref[piece].astype(F32)
        square = total[2 * units : 2 * units + 1] + total[2 * units + 1 : 2 * units + 2]
        scale = lax.rsqrt(square * (1.0 / d) + EPS)
        gate = total[:units] * scale
        up = total[units : 2 * units] * scale
        hidden = (gate / (1.0 + jnp.exp(-gate)) * up).astype(BF16)
        for to in range(count):
            out_ref[to] = hidden

    return pl.pallas_call(
        kernel,
        out_shape=jax.ShapeDtypeStruct((count, units, tokens), BF16),
        in_specs=[vmem()],
        out_specs=vmem(),
        compiler_params=pltpu.CompilerParams(vmem_limit_bytes=4 * 1024 * 1024),
        name="activate",
    )(parts)


def gate_up(own, other, pieces, at):
    blocks, rows, half = own.shape
    part = rows - EXTRA
    both, depth = pieces[0].shape

    def kernel(at_ref, own_ref, other_ref, *rest):
        piece_refs, out_ref, carried_ref = rest[:Y], rest[Y], rest[Y + 1]
        weights, rhs, tails, sem = rest[Y + 2 :]
        y, core, mine = at_ref[0], at_ref[1], at_ref[2]
        copies = []
        for shift in range(Y):
            to = lax.rem(y - shift + Y, Y)
            place = pl.ds(pl.multiple_of(to * both, both), both)
            copies.append(
                pltpu.make_async_copy(piece_refs[shift], weights.at[place, :], sem.at[shift])
            )
        for copy in copies:
            copy.start()
        for turn, ref in enumerate((own_ref, other_ref)):
            side = core if turn == 0 else 1 - core
            place = pl.ds(pl.multiple_of(side * half, half), half)
            square = jnp.zeros((2, half), F32)
            for block in range(blocks):
                rhs[block * part : (block + 1) * part, place] = ref[block, :part, :]
                square = square + ref[block, part : part + 2, :].astype(F32)
            square = square[0:1] + square[1:2]
            high = square.astype(BF16).astype(F32)
            tails[:, place] = jnp.concatenate(
                [high, square - high, jnp.zeros((EXTRA - 2, half), F32)], axis=0
            ).astype(BF16)
            carried_ref[:, place] = ref[mine, :part, :]
        for copy in copies:
            copy.wait()
        total = jnp.dot(weights[...], rhs[...], preferred_element_type=F32)
        for to in range(Y):
            out_ref[to, :both, :] = total[to * both : (to + 1) * both].astype(BF16)
            out_ref[to, both:, :] = tails[...]

    return pl.pallas_call(
        kernel,
        out_shape=[
            jax.ShapeDtypeStruct((Y, both + EXTRA, CORES * half), BF16),
            jax.ShapeDtypeStruct((part, CORES * half), BF16),
        ],
        in_specs=[smem(), vmem(), vmem()] + [pl.BlockSpec(memory_space=pltpu.HBM)] * Y,
        out_specs=[vmem(), vmem()],
        scratch_shapes=[
            pltpu.VMEM((Y * both, depth), BF16),
            pltpu.VMEM((depth, CORES * half), BF16),
            pltpu.VMEM((EXTRA, CORES * half), BF16),
            pltpu.SemaphoreType.DMA((Y,)),
        ],
        compiler_params=pltpu.CompilerParams(vmem_limit_bytes=8 * 1024 * 1024),
        name="gate_up",
    )(at, own, other, *pieces)


def shards(attention_out, w_out, residual, norm_gain, w_gate, w_up, w_down):
    x_at = lax.axis_index("x")
    zl_at = lax.axis_index("zl")
    core_at = lax.axis_index("core")
    y_at = lax.axis_index("y")
    zh_at = lax.axis_index("zh")
    d = residual.shape[1]
    t_rows, heads = attention_out.shape
    cols = w_out.shape[1]
    units = w_gate.shape[0]
    blocks = X * ZL
    half = t_rows * blocks
    tokens = half * CORES
    part = CORES * cols // Y

    cut = cut_weights(w_gate, w_up, norm_gain, y_at)
    first_piece, third_piece = shift_y(cut[1], 1), shift_y(cut[3], 3)
    w_other = swap_cores(w_out)
    first = core_at == 0
    w_pair = jnp.concatenate(
        [jnp.where(first, w_out, w_other), jnp.where(first, w_other, w_out)], axis=1
    )

    got = exchange(pack_rows(attention_out, residual), ("x", "zl"))
    att = got[:, :t_rows].reshape(half, heads)
    res = got[:, t_rows]
    token = lax.broadcasted_iota(jnp.int32, (blocks, half), 1)
    source = lax.broadcasted_iota(jnp.int32, (blocks, half), 0)
    place = (token == source * t_rows + (y_at * ZH + zh_at)).astype(BF16)
    partial = lax.dot_general(
        w_pair, att, (((0,), (1,)), ((), ())), preferred_element_type=F32
    ) + lax.dot_general(res, place, (((0,), (0,)), ((), ())), preferred_element_type=F32)
    partial = partial.astype(BF16).reshape(Y, part, half)
    partial, first_piece, third_piece, cut = lax.optimization_barrier(
        (partial, first_piece, third_piece, cut)
    )
    by_y = exchange(partial, "y")
    over_y, cut = lax.optimization_barrier((sum_and_replicate(by_y, ZH), cut))
    second_piece = shift_y(cut[2], 2)
    by_zh = exchange(over_y, "zh")
    by_zh, second_piece = lax.optimization_barrier((by_zh, second_piece))
    pieces = [cut[0], first_piece, second_piece, third_piece]
    spread = exchange(carried_and_squares(by_zh, ZL), "zl")
    spread = exchange(replicate(spread, X), "x")
    spread = spread.reshape(blocks, part + EXTRA, half)
    outs, kept = gate_up(
        spread,
        swap_cores(spread),
        pieces,
        jnp.stack([y_at, core_at, x_at * ZL + zl_at]),
    )
    hidden = exchange(activate(exchange(outs, "y"), d, ZL), "zl")
    hidden = exchange(replicate(hidden, X), "x")
    hidden = hidden.reshape(blocks, units, tokens)
    hidden_pair = (hidden, swap_cores(hidden))
    down_w = w_down.reshape(blocks, CORES, units, cols)
    feature = lax.broadcasted_iota(jnp.int32, (part, cols), 0)
    column = lax.broadcasted_iota(jnp.int32, (part, cols), 1)
    adds = (y_at // 2 == core_at) & (zh_at == 0)
    keep = ((column == feature + (y_at % 2) * part) & adds).astype(BF16)
    down = lax.dot_general(kept, keep, (((0,), (0,)), ((), ())), preferred_element_type=F32)
    for turn in range(CORES):
        side = core_at if turn == 0 else 1 - core_at
        down = down + lax.dot_general(
            hidden_pair[turn].reshape(blocks * units, tokens),
            lax.dynamic_index_in_dim(down_w, side, 1, keepdims=False).reshape(
                blocks * units, cols
            ),
            (((0,), (0,)), ((), ())),
            preferred_element_type=F32,
        )
    by_owner = jnp.transpose(
        down.astype(BF16).reshape(CORES, X, ZL, Y, ZH, cols), (1, 3, 0, 2, 4, 5)
    ).reshape(X * Y, CORES * ZL * ZH, cols)
    near = exchange(by_owner, ("x", "y")).reshape(X, Y, CORES * ZL * ZH, cols)
    near = jnp.sum(near.astype(F32), axis=1).astype(BF16)
    near = jnp.transpose(near, (1, 0, 2)).reshape(CORES * ZL * ZH, X * cols // 128, 128)
    final = exchange(near, ("core", "zl", "zh"))
    final = final.reshape(CORES, ZL, ZH, X, cols).astype(F32)
    mixed = jnp.sum(final, axis=2)
    mixed = jnp.transpose(mixed, (2, 1, 0, 3)).reshape(1, d)
    return mixed.astype(BF16)


def solution(mesh):
    view = Mesh(
        mesh.devices.reshape(X, ZL, CORES, Y, ZH), ("x", "zl", "core", "y", "zh")
    )
    ctx = ("x", "zl", "core")
    tp = ("y", "zh")
    in_specs = (
        P(ctx, tp),
        P(tp, ctx),
        P(ctx + tp, None),
        P(),
        P(ctx + tp, None),
        P(ctx + tp, None),
        P(None, tp, ctx),
    )
    return jax.shard_map(
        shards, mesh=view, in_specs=in_specs, out_specs=P(ctx + tp, None), check_vma=False
    )
```

```python
import jax
import jax.numpy as jnp
from jax import lax
from jax.experimental import pallas as pl
from jax.experimental.pallas import tpu as pltpu
from jax.sharding import Mesh, PartitionSpec as P

F32 = jnp.float32
BF16 = jnp.bfloat16
EPS = 1e-05
X, ZL, Y, ZH = 4, 4, 4, 4
CORES = 2
EXTRA = 16


def exchange(value, axes):
    return lax.all_to_all(value, axes, 0, 0, tiled=True)


def replicate(value, count):
    return lax.optimization_barrier(jnp.broadcast_to(value[None], (count,) + value.shape))


def swap_cores(value):
    return lax.ppermute(value, "core", [(0, 1), (1, 0)])


def shift_along(value, axis, shift):
    return lax.ppermute(value, axis, [(i, (i + shift) % 4) for i in range(4)])


def vmem():
    return pl.BlockSpec(memory_space=pltpu.VMEM)


def smem():
    return pl.BlockSpec(memory_space=pltpu.SMEM)


def pack_rows(attention_out, residual):
    t_rows, heads = attention_out.shape
    wide = residual.shape[1] // (X * ZL)
    rows = 24

    def kernel(att_ref, res_ref, sent_ref):
        for to in range(X * ZL):
            sent_ref[to, :t_rows, :] = att_ref[...]
            sent_ref[to, t_rows:, :] = jnp.zeros((rows - t_rows, heads), BF16)
            sent_ref[to, t_rows : t_rows + 1, :] = res_ref[:, to * wide : (to + 1) * wide]

    return pl.pallas_call(
        kernel,
        out_shape=jax.ShapeDtypeStruct((X * ZL, rows, heads), BF16),
        in_specs=[vmem(), vmem()],
        out_specs=vmem(),
        compiler_params=pltpu.CompilerParams(vmem_limit_bytes=4 * 1024 * 1024),
        name="pack_rows",
    )(attention_out, residual)


def cut_weights(w_gate, w_up, norm_gain, y_at):
    units, d = w_gate.shape
    blocks = X * ZL
    wide = d // blocks
    part = wide // Y

    def kernel(at_ref, gate_ref, up_ref, gain_ref, *piece_refs):
        for shift in range(Y):
            to = lax.rem(at_ref[0] + shift, Y)
            for block in range(blocks):
                place = pl.ds(pl.multiple_of(block * wide + to * part, part), part)
                gain = gain_ref[:, place]
                both = jnp.concatenate(
                    [gate_ref[:, place].astype(F32) * gain, up_ref[:, place].astype(F32) * gain],
                    axis=0,
                )
                piece_refs[shift][:, block * part : (block + 1) * part] = both.astype(BF16)

    return pl.pallas_call(
        kernel,
        out_shape=[jax.ShapeDtypeStruct((2 * units, blocks * part), BF16)] * Y,
        in_specs=[smem(), vmem(), vmem(), vmem()],
        out_specs=[vmem()] * Y,
        compiler_params=pltpu.CompilerParams(vmem_limit_bytes=12 * 1024 * 1024),
        name="cut_weights",
    )(y_at.reshape(1), w_gate, w_up, norm_gain.reshape(1, d))


def project(got, w_out, w_other, at):
    blocks, _, heads = got.shape
    cols = w_out.shape[1]
    t_rows = Y * ZH
    half = blocks * t_rows
    part = CORES * cols // Y

    def kernel(at_ref, got_ref, own_ref, other_ref, out_ref, att, res):
        y, zh, core = at_ref[0], at_ref[1], at_ref[2]
        for x in range(X):
            for zl in range(ZL):
                block = x * ZL + zl
                for row in range(Y):
                    to = ((x * Y + row) * ZL + zl) * ZH
                    att[to : to + ZH, :] = got_ref[block, row * ZH : (row + 1) * ZH, :]
                res[block : block + 1, :] = got_ref[block, t_rows : t_rows + 1, :]
        token = lax.broadcasted_iota(jnp.int32, (half, blocks), 0)
        source = lax.broadcasted_iota(jnp.int32, (half, blocks), 1)
        place = ((source // ZL) * Y + y) * t_rows + lax.rem(source, ZL) * ZH + zh
        pick = jnp.where(token == place, 1.0, 0.0).astype(BF16)
        for turn, ref in enumerate((own_ref, other_ref)):
            side = core if turn == 0 else 1 - core
            columns = pl.ds(pl.multiple_of(side * cols, cols), cols)
            total = jnp.dot(att[...], ref[...], preferred_element_type=F32) + jnp.dot(
                pick, res[:, columns], preferred_element_type=F32
            )
            total = total.T.astype(BF16)
            for piece in range(cols // part):
                out_ref[side * (cols // part) + piece] = total[piece * part : (piece + 1) * part]

    return pl.pallas_call(
        kernel,
        out_shape=jax.ShapeDtypeStruct((Y, part, half), BF16),
        in_specs=[smem(), vmem(), vmem(), vmem()],
        out_specs=vmem(),
        scratch_shapes=[pltpu.VMEM((half, heads), BF16), pltpu.VMEM((blocks, heads), BF16)],
        compiler_params=pltpu.CompilerParams(vmem_limit_bytes=6 * 1024 * 1024),
        name="project",
    )(at, got, w_out, w_other)


def down(hidden, pieces, kept, at):
    depth, tokens = hidden.shape
    cols = pieces[0].shape[1]
    part = kept.shape[0]
    near = tokens // (X * Y * CORES)

    def kernel(at_ref, hidden_ref, kept_ref, *rest):
        piece_refs, out_ref = rest[:X], rest[X]
        x, y, core, zh = at_ref[0], at_ref[1], at_ref[2], at_ref[3]
        rows = hidden_ref[...].astype(F32)
        units = depth // (CORES * ZL)
        rows = jnp.concatenate(
            [
                rows[(side * ZL + zl) * units : (side * ZL + zl + 1) * units]
                for zl in range(ZL)
                for side in range(CORES)
            ],
            axis=0,
        )
        lhs = rows.T.astype(BF16)
        kept_rows = kept_ref[...].astype(F32).T
        adds = (y // 2 == core) & (zh == 0)
        left = jnp.where(adds & (lax.rem(y, 2) == 0), 1.0, 0.0)
        right = jnp.where(adds & (lax.rem(y, 2) == 1), 1.0, 0.0)
        for shift in range(X):
            total = jnp.dot(lhs, piece_refs[shift][...], preferred_element_type=F32)
            if shift == 0:
                total = total + jnp.concatenate([kept_rows * left, kept_rows * right], axis=1)
            total = total.astype(BF16)
            start = lax.rem(x - shift + X, X) * cols
            place = pl.ds(pl.multiple_of(start, cols), cols)
            for side in range(CORES):
                for to in range(X * Y):
                    row = side * (tokens // CORES) + to * near
                    out_ref[to, side * near : (side + 1) * near, place] = total[row : row + near]

    return pl.pallas_call(
        kernel,
        out_shape=jax.ShapeDtypeStruct((X * Y, CORES * near, X * cols), BF16),
        in_specs=[smem(), vmem(), vmem()] + [vmem()] * X,
        out_specs=vmem(),
        compiler_params=pltpu.CompilerParams(vmem_limit_bytes=10 * 1024 * 1024),
        name="down",
    )(at, hidden, kept, *pieces)


def sum_and_replicate(parts, count):
    pieces, rows, width = parts.shape

    def kernel(parts_ref, out_ref):
        total = parts_ref[0].astype(F32)
        for piece in range(1, pieces):
            total = total + parts_ref[piece].astype(F32)
        for to in range(count):
            out_ref[to] = total.astype(BF16)

    return pl.pallas_call(
        kernel,
        out_shape=jax.ShapeDtypeStruct((count, rows, width), BF16),
        in_specs=[vmem()],
        out_specs=vmem(),
        compiler_params=pltpu.CompilerParams(vmem_limit_bytes=4 * 1024 * 1024),
        name="sum_and_replicate",
    )(parts)


def carried_and_squares(parts, count):
    pieces, rows, width = parts.shape

    def kernel(parts_ref, out_ref):
        total = parts_ref[0].astype(F32)
        for piece in range(1, pieces):
            total = total + parts_ref[piece].astype(F32)
        square = jnp.sum(total * total, axis=0, keepdims=True)
        high = square.astype(BF16).astype(F32)
        tail = jnp.concatenate(
            [high, square - high, jnp.zeros((EXTRA - 2, width), F32)], axis=0
        ).astype(BF16)
        for to in range(count):
            out_ref[to, :rows, :] = total.astype(BF16)
            out_ref[to, rows:, :] = tail

    return pl.pallas_call(
        kernel,
        out_shape=jax.ShapeDtypeStruct((count, rows + EXTRA, width), BF16),
        in_specs=[vmem()],
        out_specs=vmem(),
        compiler_params=pltpu.CompilerParams(vmem_limit_bytes=4 * 1024 * 1024),
        name="carried_and_squares",
    )(parts)


def activate(parts, d, count):
    pieces, rows, tokens = parts.shape
    units = (rows - EXTRA) // 2

    def kernel(parts_ref, out_ref):
        total = parts_ref[0].astype(F32)
        for piece in range(1, pieces):
            total = total + parts_ref[piece].astype(F32)
        square = total[2 * units : 2 * units + 1] + total[2 * units + 1 : 2 * units + 2]
        scale = lax.rsqrt(square * (1.0 / d) + EPS)
        gate = total[:units] * scale
        up = total[units : 2 * units] * scale
        hidden = (gate / (1.0 + jnp.exp(-gate)) * up).astype(BF16)
        for to in range(count):
            out_ref[to] = hidden

    return pl.pallas_call(
        kernel,
        out_shape=jax.ShapeDtypeStruct((count, units, tokens), BF16),
        in_specs=[vmem()],
        out_specs=vmem(),
        compiler_params=pltpu.CompilerParams(vmem_limit_bytes=4 * 1024 * 1024),
        name="activate",
    )(parts)


def gate_up(own, other, pieces, at):
    blocks, rows, half = own.shape
    part = rows - EXTRA
    both, depth = pieces[0].shape

    def kernel(at_ref, own_ref, other_ref, *rest):
        piece_refs, out_ref, carried_ref = rest[:Y], rest[Y], rest[Y + 1]
        weights, rhs, tails = rest[Y + 2 :]
        y, core, mine = at_ref[0], at_ref[1], at_ref[2]
        for shift in range(Y):
            to = lax.rem(y - shift + Y, Y)
            weights[pl.ds(pl.multiple_of(to * both, both), both), :] = piece_refs[shift][...]
        for turn, ref in enumerate((own_ref, other_ref)):
            side = core if turn == 0 else 1 - core
            place = pl.ds(pl.multiple_of(side * half, half), half)
            square = jnp.zeros((2, half), F32)
            for block in range(blocks):
                rhs[block * part : (block + 1) * part, place] = ref[block, :part, :]
                square = square + ref[block, part : part + 2, :].astype(F32)
            square = square[0:1] + square[1:2]
            high = square.astype(BF16).astype(F32)
            tails[:, place] = jnp.concatenate(
                [high, square - high, jnp.zeros((EXTRA - 2, half), F32)], axis=0
            ).astype(BF16)
            carried_ref[:, place] = ref[mine, :part, :]
        total = jnp.dot(weights[...], rhs[...], preferred_element_type=F32)
        for to in range(Y):
            out_ref[to, :both, :] = total[to * both : (to + 1) * both].astype(BF16)
            out_ref[to, both:, :] = tails[...]

    return pl.pallas_call(
        kernel,
        out_shape=[
            jax.ShapeDtypeStruct((Y, both + EXTRA, CORES * half), BF16),
            jax.ShapeDtypeStruct((part, CORES * half), BF16),
        ],
        in_specs=[smem(), vmem(), vmem()] + [vmem()] * Y,
        out_specs=[vmem(), vmem()],
        scratch_shapes=[
            pltpu.VMEM((Y * both, depth), BF16),
            pltpu.VMEM((depth, CORES * half), BF16),
            pltpu.VMEM((EXTRA, CORES * half), BF16),
        ],
        compiler_params=pltpu.CompilerParams(vmem_limit_bytes=8 * 1024 * 1024),
        name="gate_up",
    )(at, own, other, *pieces)


def shards(attention_out, w_out, residual, norm_gain, w_gate, w_up, w_down):
    x_at = lax.axis_index("x")
    zl_at = lax.axis_index("zl")
    core_at = lax.axis_index("core")
    y_at = lax.axis_index("y")
    zh_at = lax.axis_index("zh")
    d = residual.shape[1]
    t_rows = attention_out.shape[0]
    cols = w_out.shape[1]
    units = w_gate.shape[0]
    blocks = X * ZL
    half = t_rows * blocks
    tokens = half * CORES
    part = CORES * cols // Y

    cut = cut_weights(w_gate, w_up, norm_gain, y_at)
    first_piece, third_piece = shift_along(cut[1], "y", 1), shift_along(cut[3], "y", 3)
    by_x = w_down.reshape(X, ZL * CORES * units, cols)
    down_cut = [
        lax.dynamic_index_in_dim(by_x, (x_at + shift) % X, 0, keepdims=False)
        for shift in range(X)
    ]
    w_other = swap_cores(w_out)

    got = exchange(pack_rows(attention_out, residual), ("x", "zl"))
    partial = project(got, w_out, w_other, jnp.stack([y_at, zh_at, core_at]))
    partial, first_piece, third_piece, cut, down_cut = lax.optimization_barrier(
        (partial, first_piece, third_piece, cut, down_cut)
    )
    by_y = exchange(partial, "y")
    over_y, cut, down_cut = lax.optimization_barrier(
        (sum_and_replicate(by_y, ZH), cut, down_cut)
    )
    second_piece = shift_along(cut[2], "y", 2)
    down_pieces = [down_cut[0]] + [
        shift_along(down_cut[shift], "x", shift) for shift in range(1, X)
    ]
    by_zh = exchange(over_y, "zh")
    by_zh, second_piece, down_pieces = lax.optimization_barrier(
        (by_zh, second_piece, down_pieces)
    )
    pieces = [cut[0], first_piece, second_piece, third_piece]
    spread = exchange(carried_and_squares(by_zh, ZL), "zl")
    spread = exchange(replicate(spread, X), "x")
    spread = spread.reshape(blocks, part + EXTRA, half)
    outs, kept = gate_up(
        spread,
        swap_cores(spread),
        pieces,
        jnp.stack([y_at, core_at, x_at * ZL + zl_at]),
    )
    hidden = exchange(activate(exchange(outs, "y"), d, ZL), "zl")
    hidden = lax.all_gather(hidden, "core", axis=0, tiled=False)
    by_owner = down(
        hidden.reshape(CORES * ZL * units, tokens),
        down_pieces,
        kept,
        jnp.stack([x_at, y_at, core_at, zh_at]),
    )
    near = sum_and_replicate(exchange(by_owner, ("x", "y")), 1)
    near = near.reshape(CORES * ZL * ZH, X * cols // 128, 128)
    final = exchange(near, ("core", "zl", "zh"))
    final = final.reshape(CORES, ZL, ZH, X, cols).astype(F32)
    mixed = jnp.sum(final, axis=2)
    mixed = jnp.transpose(mixed, (2, 1, 0, 3)).reshape(1, d)
    return mixed.astype(BF16)


def solution(mesh):
    view = Mesh(
        mesh.devices.reshape(X, ZL, CORES, Y, ZH), ("x", "zl", "core", "y", "zh")
    )
    ctx = ("x", "zl", "core")
    tp = ("y", "zh")
    in_specs = (
        P(ctx, tp),
        P(tp, ctx),
        P(ctx + tp, None),
        P(),
        P(ctx + tp, None),
        P(ctx + tp, None),
        P(None, tp, ctx),
    )
    return jax.shard_map(
        shards, mesh=view, in_specs=in_specs, out_specs=P(ctx + tp, None), check_vma=False
    )
```

```python
import jax
import jax.numpy as jnp
from jax import lax
from jax.experimental import pallas as pl
from jax.experimental.pallas import tpu as pltpu
from jax.sharding import Mesh, PartitionSpec as P

F32 = jnp.float32
BF16 = jnp.bfloat16
EPS = 1e-05
X, ZL, Y, ZH = 4, 4, 4, 4
CORES = 2
EXTRA = 16


def exchange(value, axes):
    return lax.all_to_all(value, axes, 0, 0, tiled=True)


def replicate(value, count):
    return lax.optimization_barrier(jnp.broadcast_to(value[None], (count,) + value.shape))


def swap_cores(value):
    return lax.ppermute(value, "core", [(0, 1), (1, 0)])


def shift_along(value, axis, shift):
    return lax.ppermute(value, axis, [(i, (i + shift) % 4) for i in range(4)])


def vmem():
    return pl.BlockSpec(memory_space=pltpu.VMEM)


def smem():
    return pl.BlockSpec(memory_space=pltpu.SMEM)


def pack_rows(attention_out, residual):
    t_rows, heads = attention_out.shape
    wide = residual.shape[1] // (X * ZL)
    rows = 24

    def kernel(att_ref, res_ref, sent_ref):
        for to in range(X * ZL):
            sent_ref[to, :t_rows, :] = att_ref[...]
            sent_ref[to, t_rows:, :] = jnp.zeros((rows - t_rows, heads), BF16)
            sent_ref[to, t_rows : t_rows + 1, :] = res_ref[:, to * wide : (to + 1) * wide]

    return pl.pallas_call(
        kernel,
        out_shape=jax.ShapeDtypeStruct((X * ZL, rows, heads), BF16),
        in_specs=[vmem(), vmem()],
        out_specs=vmem(),
        compiler_params=pltpu.CompilerParams(vmem_limit_bytes=4 * 1024 * 1024),
        name="pack_rows",
    )(attention_out, residual)


def cut_weights(w_gate, w_up, norm_gain, y_at):
    units, d = w_gate.shape
    blocks = X * ZL
    wide = d // blocks
    part = wide // Y

    def kernel(at_ref, gate_ref, up_ref, gain_ref, *piece_refs):
        for shift in range(Y):
            to = lax.rem(at_ref[0] + shift, Y)
            for block in range(blocks):
                place = pl.ds(pl.multiple_of(block * wide + to * part, part), part)
                gain = gain_ref[:, place]
                both = jnp.concatenate(
                    [gate_ref[:, place].astype(F32) * gain, up_ref[:, place].astype(F32) * gain],
                    axis=0,
                )
                piece_refs[shift][:, block * part : (block + 1) * part] = both.astype(BF16)

    return pl.pallas_call(
        kernel,
        out_shape=[jax.ShapeDtypeStruct((2 * units, blocks * part), BF16)] * Y,
        in_specs=[smem(), vmem(), vmem(), vmem()],
        out_specs=[vmem()] * Y,
        compiler_params=pltpu.CompilerParams(vmem_limit_bytes=12 * 1024 * 1024),
        name="cut_weights",
    )(y_at.reshape(1), w_gate, w_up, norm_gain.reshape(1, d))


def project(got, w_out, w_other, at):
    blocks, _, heads = got.shape
    cols = w_out.shape[1]
    t_rows = Y * ZH
    half = blocks * t_rows
    part = CORES * cols // Y

    def kernel(at_ref, got_ref, own_ref, other_ref, out_ref, att, res):
        y, zh, core = at_ref[0], at_ref[1], at_ref[2]
        for x in range(X):
            for zl in range(ZL):
                block = x * ZL + zl
                for row in range(Y):
                    to = ((x * Y + row) * ZL + zl) * ZH
                    att[to : to + ZH, :] = got_ref[block, row * ZH : (row + 1) * ZH, :]
                res[block : block + 1, :] = got_ref[block, t_rows : t_rows + 1, :]
        token = lax.broadcasted_iota(jnp.int32, (half, blocks), 0)
        source = lax.broadcasted_iota(jnp.int32, (half, blocks), 1)
        place = ((source // ZL) * Y + y) * t_rows + lax.rem(source, ZL) * ZH + zh
        pick = jnp.where(token == place, 1.0, 0.0).astype(BF16)
        for turn, ref in enumerate((own_ref, other_ref)):
            side = core if turn == 0 else 1 - core
            columns = pl.ds(pl.multiple_of(side * cols, cols), cols)
            total = jnp.dot(att[...], ref[...], preferred_element_type=F32) + jnp.dot(
                pick, res[:, columns], preferred_element_type=F32
            )
            total = total.T.astype(BF16)
            for piece in range(cols // part):
                out_ref[side * (cols // part) + piece] = total[piece * part : (piece + 1) * part]

    return pl.pallas_call(
        kernel,
        out_shape=jax.ShapeDtypeStruct((Y, part, half), BF16),
        in_specs=[smem(), vmem(), vmem(), vmem()],
        out_specs=vmem(),
        scratch_shapes=[pltpu.VMEM((half, heads), BF16), pltpu.VMEM((blocks, heads), BF16)],
        compiler_params=pltpu.CompilerParams(vmem_limit_bytes=6 * 1024 * 1024),
        name="project",
    )(at, got, w_out, w_other)


def down(hidden, pieces, kept, at):
    depth, tokens = hidden.shape
    cols = pieces[0].shape[1]
    part = kept.shape[0]
    near = tokens // (X * Y * CORES)

    def kernel(at_ref, hidden_ref, kept_ref, *rest):
        piece_refs, out_ref = rest[:X], rest[X]
        x, y, core, zh = at_ref[0], at_ref[1], at_ref[2], at_ref[3]
        rows = hidden_ref[...].astype(F32)
        units = depth // (CORES * ZL)
        rows = jnp.concatenate(
            [
                rows[(side * ZL + zl) * units : (side * ZL + zl + 1) * units]
                for zl in range(ZL)
                for side in range(CORES)
            ],
            axis=0,
        )
        lhs = rows.T.astype(BF16)
        kept_rows = kept_ref[...].astype(F32).T
        adds = (y // 2 == core) & (zh == 0)
        left = jnp.where(adds & (lax.rem(y, 2) == 0), 1.0, 0.0)
        right = jnp.where(adds & (lax.rem(y, 2) == 1), 1.0, 0.0)
        for shift in range(X):
            total = jnp.dot(lhs, piece_refs[shift][...], preferred_element_type=F32)
            if shift == 0:
                total = total + jnp.concatenate([kept_rows * left, kept_rows * right], axis=1)
            total = total.astype(BF16)
            start = lax.rem(x - shift + X, X) * cols
            place = pl.ds(pl.multiple_of(start, cols), cols)
            for side in range(CORES):
                for to in range(X * Y):
                    row = side * (tokens // CORES) + to * near
                    out_ref[to, side * near : (side + 1) * near, place] = total[row : row + near]

    return pl.pallas_call(
        kernel,
        out_shape=jax.ShapeDtypeStruct((X * Y, CORES * near, X * cols), BF16),
        in_specs=[smem(), vmem(), vmem()] + [vmem()] * X,
        out_specs=vmem(),
        compiler_params=pltpu.CompilerParams(vmem_limit_bytes=10 * 1024 * 1024),
        name="down",
    )(at, hidden, kept, *pieces)


def sum_and_replicate(parts, count):
    pieces, rows, width = parts.shape

    def kernel(parts_ref, out_ref):
        total = parts_ref[0].astype(F32)
        for piece in range(1, pieces):
            total = total + parts_ref[piece].astype(F32)
        for to in range(count):
            out_ref[to] = total.astype(BF16)

    return pl.pallas_call(
        kernel,
        out_shape=jax.ShapeDtypeStruct((count, rows, width), BF16),
        in_specs=[vmem()],
        out_specs=vmem(),
        compiler_params=pltpu.CompilerParams(vmem_limit_bytes=4 * 1024 * 1024),
        name="sum_and_replicate",
    )(parts)


def carried_and_squares(parts, count):
    pieces, rows, width = parts.shape

    def kernel(parts_ref, out_ref):
        total = parts_ref[0].astype(F32)
        for piece in range(1, pieces):
            total = total + parts_ref[piece].astype(F32)
        square = jnp.sum(total * total, axis=0, keepdims=True)
        high = square.astype(BF16).astype(F32)
        tail = jnp.concatenate(
            [high, square - high, jnp.zeros((EXTRA - 2, width), F32)], axis=0
        ).astype(BF16)
        for to in range(count):
            out_ref[to, :rows, :] = total.astype(BF16)
            out_ref[to, rows:, :] = tail

    return pl.pallas_call(
        kernel,
        out_shape=jax.ShapeDtypeStruct((count, rows + EXTRA, width), BF16),
        in_specs=[vmem()],
        out_specs=vmem(),
        compiler_params=pltpu.CompilerParams(vmem_limit_bytes=4 * 1024 * 1024),
        name="carried_and_squares",
    )(parts)


def activate(parts, d, count):
    pieces, rows, tokens = parts.shape
    units = (rows - EXTRA) // 2

    def kernel(parts_ref, out_ref):
        total = parts_ref[0].astype(F32)
        for piece in range(1, pieces):
            total = total + parts_ref[piece].astype(F32)
        square = total[2 * units : 2 * units + 1] + total[2 * units + 1 : 2 * units + 2]
        scale = lax.rsqrt(square * (1.0 / d) + EPS)
        gate = total[:units] * scale
        up = total[units : 2 * units] * scale
        hidden = (gate / (1.0 + jnp.exp(-gate)) * up).astype(BF16)
        for to in range(count):
            out_ref[to] = hidden

    return pl.pallas_call(
        kernel,
        out_shape=jax.ShapeDtypeStruct((count, units, tokens), BF16),
        in_specs=[vmem()],
        out_specs=vmem(),
        compiler_params=pltpu.CompilerParams(vmem_limit_bytes=4 * 1024 * 1024),
        name="activate",
    )(parts)


def gate_up(own, other, pieces, at):
    blocks, rows, half = own.shape
    part = rows - EXTRA
    both, depth = pieces[0].shape

    def kernel(at_ref, own_ref, other_ref, *rest):
        piece_refs, out_ref, carried_ref = rest[:Y], rest[Y], rest[Y + 1]
        weights, rhs, tails = rest[Y + 2 :]
        y, core, mine = at_ref[0], at_ref[1], at_ref[2]
        for shift in range(Y):
            to = lax.rem(y - shift + Y, Y)
            weights[pl.ds(pl.multiple_of(to * both, both), both), :] = piece_refs[shift][...]
        for turn, ref in enumerate((own_ref, other_ref)):
            side = core if turn == 0 else 1 - core
            place = pl.ds(pl.multiple_of(side * half, half), half)
            square = jnp.zeros((2, half), F32)
            for block in range(blocks):
                rhs[block * part : (block + 1) * part, place] = ref[block, :part, :]
                square = square + ref[block, part : part + 2, :].astype(F32)
            square = square[0:1] + square[1:2]
            high = square.astype(BF16).astype(F32)
            tails[:, place] = jnp.concatenate(
                [high, square - high, jnp.zeros((EXTRA - 2, half), F32)], axis=0
            ).astype(BF16)
            carried_ref[:, place] = ref[mine, :part, :]
        total = jnp.dot(weights[...], rhs[...], preferred_element_type=F32)
        for to in range(Y):
            out_ref[to, :both, :] = total[to * both : (to + 1) * both].astype(BF16)
            out_ref[to, both:, :] = tails[...]

    return pl.pallas_call(
        kernel,
        out_shape=[
            jax.ShapeDtypeStruct((Y, both + EXTRA, CORES * half), BF16),
            jax.ShapeDtypeStruct((part, CORES * half), BF16),
        ],
        in_specs=[smem(), vmem(), vmem()] + [vmem()] * Y,
        out_specs=[vmem(), vmem()],
        scratch_shapes=[
            pltpu.VMEM((Y * both, depth), BF16),
            pltpu.VMEM((depth, CORES * half), BF16),
            pltpu.VMEM((EXTRA, CORES * half), BF16),
        ],
        compiler_params=pltpu.CompilerParams(vmem_limit_bytes=8 * 1024 * 1024),
        name="gate_up",
    )(at, own, other, *pieces)


def shards(attention_out, w_out, residual, norm_gain, w_gate, w_up, w_down):
    x_at = lax.axis_index("x")
    zl_at = lax.axis_index("zl")
    core_at = lax.axis_index("core")
    y_at = lax.axis_index("y")
    zh_at = lax.axis_index("zh")
    d = residual.shape[1]
    t_rows = attention_out.shape[0]
    cols = w_out.shape[1]
    units = w_gate.shape[0]
    blocks = X * ZL
    half = t_rows * blocks
    tokens = half * CORES
    part = CORES * cols // Y

    cut = cut_weights(w_gate, w_up, norm_gain, y_at)
    first_piece, third_piece = shift_along(cut[1], "y", 1), shift_along(cut[3], "y", 3)
    by_x = w_down.reshape(X, ZL * CORES * units, cols)
    down_cut = [
        lax.dynamic_index_in_dim(by_x, (x_at + shift) % X, 0, keepdims=False)
        for shift in range(X)
    ]
    w_other = swap_cores(w_out)

    got = exchange(pack_rows(attention_out, residual), ("x", "zl"))
    partial = project(got, w_out, w_other, jnp.stack([y_at, zh_at, core_at]))
    by_y = exchange(partial, "y")
    over_y, first_piece, third_piece, cut, down_cut = lax.optimization_barrier(
        (sum_and_replicate(by_y, ZH), first_piece, third_piece, cut, down_cut)
    )
    second_piece = shift_along(cut[2], "y", 2)
    down_pieces = [down_cut[0]] + [
        shift_along(down_cut[shift], "x", shift) if shift != 2 else None for shift in range(1, X)
    ]
    by_zh = exchange(over_y, "zh")
    by_zh, second_piece, down_pieces[1], down_pieces[3], down_cut = lax.optimization_barrier(
        (by_zh, second_piece, down_pieces[1], down_pieces[3], down_cut)
    )
    down_pieces[2] = shift_along(down_cut[2], "x", 2)
    pieces = [cut[0], first_piece, second_piece, third_piece]
    spread, down_pieces[2] = lax.optimization_barrier(
        (exchange(carried_and_squares(by_zh, ZL), "zl"), down_pieces[2])
    )
    spread = exchange(replicate(spread, X), "x")
    spread = spread.reshape(blocks, part + EXTRA, half)
    outs, kept = gate_up(
        spread,
        swap_cores(spread),
        pieces,
        jnp.stack([y_at, core_at, x_at * ZL + zl_at]),
    )
    hidden = exchange(activate(exchange(outs, "y"), d, ZL), "zl")
    hidden = lax.all_gather(hidden, "core", axis=0, tiled=False)
    by_owner = down(
        hidden.reshape(CORES * ZL * units, tokens),
        down_pieces,
        kept,
        jnp.stack([x_at, y_at, core_at, zh_at]),
    )
    near = sum_and_replicate(exchange(by_owner, ("x", "y")), 1)
    near = near.reshape(CORES * ZL * ZH, X * cols // 128, 128)
    final = exchange(near, ("core", "zl", "zh"))
    final = final.reshape(CORES, ZL, ZH, X, cols).astype(F32)
    mixed = jnp.sum(final, axis=2)
    mixed = jnp.transpose(mixed, (2, 1, 0, 3)).reshape(1, d)
    return mixed.astype(BF16)


def solution(mesh):
    view = Mesh(
        mesh.devices.reshape(X, ZL, CORES, Y, ZH), ("x", "zl", "core", "y", "zh")
    )
    ctx = ("x", "zl", "core")
    tp = ("y", "zh")
    in_specs = (
        P(ctx, tp),
        P(tp, ctx),
        P(ctx + tp, None),
        P(),
        P(ctx + tp, None),
        P(ctx + tp, None),
        P(None, tp, ctx),
    )
    return jax.shard_map(
        shards, mesh=view, in_specs=in_specs, out_specs=P(ctx + tp, None), check_vma=False
    )
```

```python
import jax
import jax.numpy as jnp
from jax import lax
from jax.experimental import pallas as pl
from jax.experimental.pallas import tpu as pltpu
from jax.sharding import Mesh, PartitionSpec as P

F32 = jnp.float32
BF16 = jnp.bfloat16
EPS = 1e-05
X, ZL, Y, ZH = 4, 4, 4, 4
CORES = 2
EXTRA = 16


def exchange(value, axes):
    return lax.all_to_all(value, axes, 0, 0, tiled=True)


def replicate(value, count):
    return lax.optimization_barrier(jnp.broadcast_to(value[None], (count,) + value.shape))


def swap_cores(value):
    return lax.ppermute(value, "core", [(0, 1), (1, 0)])


def shift_along(value, axis, shift):
    return lax.ppermute(value, axis, [(i, (i + shift) % 4) for i in range(4)])


def vmem():
    return pl.BlockSpec(memory_space=pltpu.VMEM)


def smem():
    return pl.BlockSpec(memory_space=pltpu.SMEM)


def pack_rows(attention_out, residual):
    t_rows, heads = attention_out.shape
    wide = residual.shape[1] // (X * ZL)
    rows = 24

    def kernel(att_ref, res_ref, sent_ref):
        for to in range(X * ZL):
            sent_ref[to, :t_rows, :] = att_ref[...]
            sent_ref[to, t_rows:, :] = jnp.zeros((rows - t_rows, heads), BF16)
            sent_ref[to, t_rows : t_rows + 1, :] = res_ref[:, to * wide : (to + 1) * wide]

    return pl.pallas_call(
        kernel,
        out_shape=jax.ShapeDtypeStruct((X * ZL, rows, heads), BF16),
        in_specs=[vmem(), vmem()],
        out_specs=vmem(),
        compiler_params=pltpu.CompilerParams(vmem_limit_bytes=56 * 1024 * 1024),
        name="pack_rows",
    )(attention_out, residual)


def cut_weights(w_gate, w_up, norm_gain, y_at):
    units, d = w_gate.shape
    blocks = X * ZL
    wide = d // blocks
    part = wide // Y

    def kernel(at_ref, gate_ref, up_ref, gain_ref, *piece_refs):
        for shift in range(Y):
            to = lax.rem(at_ref[0] + shift, Y)
            for block in range(blocks):
                place = pl.ds(pl.multiple_of(block * wide + to * part, part), part)
                gain = gain_ref[:, place]
                both = jnp.concatenate(
                    [gate_ref[:, place].astype(F32) * gain, up_ref[:, place].astype(F32) * gain],
                    axis=0,
                )
                piece_refs[shift][:, block * part : (block + 1) * part] = both.astype(BF16)

    return pl.pallas_call(
        kernel,
        out_shape=[jax.ShapeDtypeStruct((2 * units, blocks * part), BF16)] * Y,
        in_specs=[smem(), vmem(), vmem(), vmem()],
        out_specs=[vmem()] * Y,
        compiler_params=pltpu.CompilerParams(vmem_limit_bytes=12 * 1024 * 1024),
        name="cut_weights",
    )(y_at.reshape(1), w_gate, w_up, norm_gain.reshape(1, d))


def project(got, w_out, w_other, at):
    blocks, _, heads = got.shape
    cols = w_out.shape[1]
    t_rows = Y * ZH
    half = blocks * t_rows
    part = CORES * cols // Y

    def kernel(at_ref, got_ref, own_ref, other_ref, out_ref, att, res):
        y, zh, core = at_ref[0], at_ref[1], at_ref[2]
        for x in range(X):
            for zl in range(ZL):
                block = x * ZL + zl
                for row in range(Y):
                    to = ((x * Y + row) * ZL + zl) * ZH
                    att[to : to + ZH, :] = got_ref[block, row * ZH : (row + 1) * ZH, :]
                res[block : block + 1, :] = got_ref[block, t_rows : t_rows + 1, :]
        token = lax.broadcasted_iota(jnp.int32, (half, blocks), 0)
        source = lax.broadcasted_iota(jnp.int32, (half, blocks), 1)
        place = ((source // ZL) * Y + y) * t_rows + lax.rem(source, ZL) * ZH + zh
        pick = jnp.where(token == place, 1.0, 0.0).astype(BF16)
        for turn, ref in enumerate((own_ref, other_ref)):
            side = core if turn == 0 else 1 - core
            columns = pl.ds(pl.multiple_of(side * cols, cols), cols)
            total = jnp.dot(att[...], ref[...], preferred_element_type=F32) + jnp.dot(
                pick, res[:, columns], preferred_element_type=F32
            )
            total = total.T.astype(BF16)
            for piece in range(cols // part):
                out_ref[side * (cols // part) + piece] = total[piece * part : (piece + 1) * part]

    return pl.pallas_call(
        kernel,
        out_shape=jax.ShapeDtypeStruct((Y, part, half), BF16),
        in_specs=[smem(), vmem(), vmem(), vmem()],
        out_specs=vmem(),
        scratch_shapes=[pltpu.VMEM((half, heads), BF16), pltpu.VMEM((blocks, heads), BF16)],
        compiler_params=pltpu.CompilerParams(vmem_limit_bytes=6 * 1024 * 1024),
        name="project",
    )(at, got, w_out, w_other)


def down(hidden, pieces, kept, at):
    depth, tokens = hidden.shape
    cols = pieces[0].shape[1]
    part = kept.shape[0]
    near = tokens // (X * Y * CORES)

    def kernel(at_ref, hidden_ref, kept_ref, *rest):
        piece_refs, out_ref = rest[:X], rest[X]
        x, y, core, zh = at_ref[0], at_ref[1], at_ref[2], at_ref[3]
        rows = hidden_ref[...].astype(F32)
        units = depth // (CORES * ZL)
        rows = jnp.concatenate(
            [
                rows[(side * ZL + zl) * units : (side * ZL + zl + 1) * units]
                for zl in range(ZL)
                for side in range(CORES)
            ],
            axis=0,
        )
        lhs = rows.T.astype(BF16)
        kept_rows = kept_ref[...].astype(F32).T
        adds = (y // 2 == core) & (zh == 0)
        left = jnp.where(adds & (lax.rem(y, 2) == 0), 1.0, 0.0)
        right = jnp.where(adds & (lax.rem(y, 2) == 1), 1.0, 0.0)
        for shift in range(X):
            total = jnp.dot(lhs, piece_refs[shift][...], preferred_element_type=F32)
            if shift == 0:
                total = total + jnp.concatenate([kept_rows * left, kept_rows * right], axis=1)
            total = total.astype(BF16)
            start = lax.rem(x - shift + X, X) * cols
            place = pl.ds(pl.multiple_of(start, cols), cols)
            for side in range(CORES):
                for to in range(X * Y):
                    row = side * (tokens // CORES) + to * near
                    out_ref[to, side * near : (side + 1) * near, place] = total[row : row + near]

    return pl.pallas_call(
        kernel,
        out_shape=jax.ShapeDtypeStruct((X * Y, CORES * near, X * cols), BF16),
        in_specs=[smem(), vmem(), vmem()] + [vmem()] * X,
        out_specs=vmem(),
        compiler_params=pltpu.CompilerParams(vmem_limit_bytes=10 * 1024 * 1024),
        name="down",
    )(at, hidden, kept, *pieces)


def sum_and_replicate(parts, count):
    pieces, rows, width = parts.shape

    def kernel(parts_ref, out_ref):
        total = parts_ref[0].astype(F32)
        for piece in range(1, pieces):
            total = total + parts_ref[piece].astype(F32)
        for to in range(count):
            out_ref[to] = total.astype(BF16)

    return pl.pallas_call(
        kernel,
        out_shape=jax.ShapeDtypeStruct((count, rows, width), BF16),
        in_specs=[vmem()],
        out_specs=vmem(),
        compiler_params=pltpu.CompilerParams(vmem_limit_bytes=4 * 1024 * 1024),
        name="sum_and_replicate",
    )(parts)


def carried_and_squares(parts, count):
    pieces, rows, width = parts.shape

    def kernel(parts_ref, out_ref):
        total = parts_ref[0].astype(F32)
        for piece in range(1, pieces):
            total = total + parts_ref[piece].astype(F32)
        square = jnp.sum(total * total, axis=0, keepdims=True)
        high = square.astype(BF16).astype(F32)
        tail = jnp.concatenate(
            [high, square - high, jnp.zeros((EXTRA - 2, width), F32)], axis=0
        ).astype(BF16)
        for to in range(count):
            out_ref[to, :rows, :] = total.astype(BF16)
            out_ref[to, rows:, :] = tail

    return pl.pallas_call(
        kernel,
        out_shape=jax.ShapeDtypeStruct((count, rows + EXTRA, width), BF16),
        in_specs=[vmem()],
        out_specs=vmem(),
        compiler_params=pltpu.CompilerParams(vmem_limit_bytes=4 * 1024 * 1024),
        name="carried_and_squares",
    )(parts)


def activate(parts, d, count):
    pieces, rows, tokens = parts.shape
    units = (rows - EXTRA) // 2

    def kernel(parts_ref, out_ref):
        total = parts_ref[0].astype(F32)
        for piece in range(1, pieces):
            total = total + parts_ref[piece].astype(F32)
        square = total[2 * units : 2 * units + 1] + total[2 * units + 1 : 2 * units + 2]
        scale = lax.rsqrt(square * (1.0 / d) + EPS)
        gate = total[:units] * scale
        up = total[units : 2 * units] * scale
        hidden = (gate / (1.0 + jnp.exp(-gate)) * up).astype(BF16)
        for to in range(count):
            out_ref[to] = hidden

    return pl.pallas_call(
        kernel,
        out_shape=jax.ShapeDtypeStruct((count, units, tokens), BF16),
        in_specs=[vmem()],
        out_specs=vmem(),
        compiler_params=pltpu.CompilerParams(vmem_limit_bytes=4 * 1024 * 1024),
        name="activate",
    )(parts)


def gate_up(spread, pieces, at, done=None):
    blocks, rows, half = spread.shape
    part = rows - EXTRA
    both, depth = pieces[0].shape
    width = half if done is None else CORES * half

    def kernel(at_ref, spread_ref, *rest):
        piece_refs, rest = rest[:Y], rest[Y:]
        if done is not None:
            done_refs, rest = rest[:2], rest[2:]
        out_ref, carried_ref, weights, rhs = rest
        y, core, mine = at_ref[0], at_ref[1], at_ref[2]
        place = slice(None)
        if done is not None:
            own = pl.ds(pl.multiple_of(core * half, half), half)
            place = pl.ds(pl.multiple_of((1 - core) * half, half), half)
            out_ref[:, :, own] = done_refs[0][...]
            carried_ref[:, own] = done_refs[1][...]
        for shift in range(Y):
            to = lax.rem(y - shift + Y, Y)
            weights[pl.ds(pl.multiple_of(to * both, both), both), :] = piece_refs[shift][...]
        square = jnp.zeros((2, half), F32)
        for block in range(blocks):
            rhs[block * part : (block + 1) * part, :] = spread_ref[block, :part, :]
            square = square + spread_ref[block, part : part + 2, :].astype(F32)
        square = square[0:1] + square[1:2]
        high = square.astype(BF16).astype(F32)
        tail = jnp.concatenate(
            [high, square - high, jnp.zeros((EXTRA - 2, half), F32)], axis=0
        ).astype(BF16)
        carried_ref[:, place] = spread_ref[mine, :part, :]
        total = jnp.dot(weights[...], rhs[...], preferred_element_type=F32)
        for to in range(Y):
            out_ref[to, :both, place] = total[to * both : (to + 1) * both].astype(BF16)
            out_ref[to, both:, place] = tail

    extra = () if done is None else tuple(done)
    return pl.pallas_call(
        kernel,
        out_shape=[
            jax.ShapeDtypeStruct((Y, both + EXTRA, width), BF16),
            jax.ShapeDtypeStruct((part, width), BF16),
        ],
        in_specs=[smem(), vmem()] + [vmem()] * (Y + len(extra)),
        out_specs=[vmem(), vmem()],
        scratch_shapes=[
            pltpu.VMEM((Y * both, depth), BF16),
            pltpu.VMEM((depth, half), BF16),
        ],
        compiler_params=pltpu.CompilerParams(vmem_limit_bytes=8 * 1024 * 1024),
        name="gate_up" if done is None else "gate_up_both",
    )(at, spread, *pieces, *extra)


def shards(attention_out, w_out, residual, norm_gain, w_gate, w_up, w_down):
    x_at = lax.axis_index("x")
    zl_at = lax.axis_index("zl")
    core_at = lax.axis_index("core")
    y_at = lax.axis_index("y")
    zh_at = lax.axis_index("zh")
    d = residual.shape[1]
    t_rows = attention_out.shape[0]
    cols = w_out.shape[1]
    units = w_gate.shape[0]
    blocks = X * ZL
    half = t_rows * blocks
    tokens = half * CORES
    part = CORES * cols // Y

    cut = cut_weights(w_gate, w_up, norm_gain, y_at)
    first_piece, third_piece = shift_along(cut[1], "y", 1), shift_along(cut[3], "y", 3)
    by_x = w_down.reshape(X, ZL * CORES * units, cols)
    down_cut = [
        lax.dynamic_index_in_dim(by_x, (x_at + shift) % X, 0, keepdims=False)
        for shift in range(X)
    ]
    w_other = swap_cores(w_out)

    got = exchange(pack_rows(attention_out, residual), ("x", "zl"))
    partial = project(got, w_out, w_other, jnp.stack([y_at, zh_at, core_at]))
    by_y = exchange(partial, "y")
    over_y, first_piece, third_piece, cut, down_cut = lax.optimization_barrier(
        (sum_and_replicate(by_y, ZH), first_piece, third_piece, cut, down_cut)
    )
    second_piece = shift_along(cut[2], "y", 2)
    down_pieces = [down_cut[0]] + [
        shift_along(down_cut[shift], "x", shift) if shift != 2 else None for shift in range(1, X)
    ]
    by_zh = exchange(over_y, "zh")
    by_zh, second_piece, down_pieces[1], down_pieces[3], down_cut = lax.optimization_barrier(
        (by_zh, second_piece, down_pieces[1], down_pieces[3], down_cut)
    )
    down_pieces[2] = shift_along(down_cut[2], "x", 2)
    pieces = [cut[0], first_piece, second_piece, third_piece]
    spread, down_pieces[2] = lax.optimization_barrier(
        (exchange(carried_and_squares(by_zh, ZL), "zl"), down_pieces[2])
    )
    spread = exchange(replicate(spread, X), "x")
    spread = spread.reshape(blocks, part + EXTRA, half)
    other = swap_cores(spread)
    at = jnp.stack([y_at, core_at, x_at * ZL + zl_at])
    outs, kept = gate_up(other, pieces, at, gate_up(spread, pieces, at))
    hidden = exchange(activate(exchange(outs, "y"), d, ZL), "zl")
    hidden = lax.all_gather(hidden, "core", axis=0, tiled=False)
    by_owner = down(
        hidden.reshape(CORES * ZL * units, tokens),
        down_pieces,
        kept,
        jnp.stack([x_at, y_at, core_at, zh_at]),
    )
    near = sum_and_replicate(exchange(by_owner, ("x", "y")), 1)
    near = near.reshape(CORES * ZL * ZH, X * cols // 128, 128)
    final = exchange(near, ("core", "zl", "zh"))
    final = final.reshape(CORES, ZL, ZH, X, cols).astype(F32)
    mixed = jnp.sum(final, axis=2)
    mixed = jnp.transpose(mixed, (2, 1, 0, 3)).reshape(1, d)
    return mixed.astype(BF16)


def solution(mesh):
    view = Mesh(
        mesh.devices.reshape(X, ZL, CORES, Y, ZH), ("x", "zl", "core", "y", "zh")
    )
    ctx = ("x", "zl", "core")
    tp = ("y", "zh")
    in_specs = (
        P(ctx, tp),
        P(tp, ctx),
        P(ctx + tp, None),
        P(),
        P(ctx + tp, None),
        P(ctx + tp, None),
        P(None, tp, ctx),
    )
    return jax.shard_map(
        shards, mesh=view, in_specs=in_specs, out_specs=P(ctx + tp, None), check_vma=False
    )
```

```python
import jax
import jax.numpy as jnp
from jax import lax
from jax.experimental import pallas as pl
from jax.experimental.pallas import tpu as pltpu
from jax.sharding import Mesh, PartitionSpec as P

F32 = jnp.float32
BF16 = jnp.bfloat16
EPS = 1e-05
X, ZL, Y, ZH = 4, 4, 4, 4
CORES = 2
EXTRA = 8


def exchange(value, axes):
    return lax.all_to_all(value, axes, 0, 0, tiled=True)


def replicate(value, count):
    return lax.optimization_barrier(jnp.broadcast_to(value[None], (count,) + value.shape))


def swap_cores(value):
    return lax.ppermute(value, "core", [(0, 1), (1, 0)])


def shift_along(value, axis, shift):
    return lax.ppermute(value, axis, [(i, (i + shift) % 4) for i in range(4)])


def vmem():
    return pl.BlockSpec(memory_space=pltpu.VMEM)


def smem():
    return pl.BlockSpec(memory_space=pltpu.SMEM)


def pack_rows(attention_out, residual):
    t_rows, heads = attention_out.shape
    wide = residual.shape[1] // (X * ZL)
    rows = 24

    def kernel(att_ref, res_ref, sent_ref):
        for to in range(X * ZL):
            sent_ref[to, :t_rows, :] = att_ref[...]
            sent_ref[to, t_rows:, :] = jnp.zeros((rows - t_rows, heads), BF16)
            sent_ref[to, t_rows : t_rows + 1, :] = res_ref[:, to * wide : (to + 1) * wide]

    return pl.pallas_call(
        kernel,
        out_shape=jax.ShapeDtypeStruct((X * ZL, rows, heads), BF16),
        in_specs=[vmem(), vmem()],
        out_specs=vmem(),
        compiler_params=pltpu.CompilerParams(vmem_limit_bytes=56 * 1024 * 1024),
        name="pack_rows",
    )(attention_out, residual)


def cut_weights(w_gate, w_up, norm_gain, y_at):
    units, d = w_gate.shape
    blocks = X * ZL
    wide = d // blocks
    part = wide // Y

    def kernel(at_ref, gate_ref, up_ref, gain_ref, *piece_refs):
        for shift in range(Y):
            to = lax.rem(at_ref[0] + shift, Y)
            for block in range(blocks):
                place = pl.ds(pl.multiple_of(block * wide + to * part, part), part)
                gain = gain_ref[:, place]
                both = jnp.concatenate(
                    [gate_ref[:, place].astype(F32) * gain, up_ref[:, place].astype(F32) * gain],
                    axis=0,
                )
                piece_refs[shift][:, block * part : (block + 1) * part] = both.astype(BF16)

    return pl.pallas_call(
        kernel,
        out_shape=[jax.ShapeDtypeStruct((2 * units, blocks * part), BF16)] * Y,
        in_specs=[smem(), vmem(), vmem(), vmem()],
        out_specs=[vmem()] * Y,
        compiler_params=pltpu.CompilerParams(vmem_limit_bytes=12 * 1024 * 1024),
        name="cut_weights",
    )(y_at.reshape(1), w_gate, w_up, norm_gain.reshape(1, d))


def project(got, w_out, w_other, at):
    blocks, _, heads = got.shape
    cols = w_out.shape[1]
    t_rows = Y * ZH
    half = blocks * t_rows
    part = CORES * cols // Y

    def kernel(at_ref, got_ref, own_ref, other_ref, out_ref, att, res):
        y, zh, core = at_ref[0], at_ref[1], at_ref[2]
        for x in range(X):
            for zl in range(ZL):
                block = x * ZL + zl
                for row in range(Y):
                    to = ((x * Y + row) * ZL + zl) * ZH
                    att[to : to + ZH, :] = got_ref[block, row * ZH : (row + 1) * ZH, :]
                res[block : block + 1, :] = got_ref[block, t_rows : t_rows + 1, :]
        token = lax.broadcasted_iota(jnp.int32, (half, blocks), 0)
        source = lax.broadcasted_iota(jnp.int32, (half, blocks), 1)
        place = ((source // ZL) * Y + y) * t_rows + lax.rem(source, ZL) * ZH + zh
        pick = jnp.where(token == place, 1.0, 0.0).astype(BF16)
        for turn, ref in enumerate((own_ref, other_ref)):
            side = core if turn == 0 else 1 - core
            columns = pl.ds(pl.multiple_of(side * cols, cols), cols)
            total = jnp.dot(att[...], ref[...], preferred_element_type=F32) + jnp.dot(
                pick, res[:, columns], preferred_element_type=F32
            )
            total = total.T.astype(BF16)
            for piece in range(cols // part):
                out_ref[side * (cols // part) + piece] = total[piece * part : (piece + 1) * part]

    return pl.pallas_call(
        kernel,
        out_shape=jax.ShapeDtypeStruct((Y, part, half), BF16),
        in_specs=[smem(), vmem(), vmem(), vmem()],
        out_specs=vmem(),
        scratch_shapes=[pltpu.VMEM((half, heads), BF16), pltpu.VMEM((blocks, heads), BF16)],
        compiler_params=pltpu.CompilerParams(vmem_limit_bytes=6 * 1024 * 1024),
        name="project",
    )(at, got, w_out, w_other)


def down(hidden, pieces, kept, at):
    depth, tokens = hidden.shape
    cols = pieces[0].shape[1]
    part = kept.shape[0]
    near = tokens // (X * Y * CORES)

    def kernel(at_ref, hidden_ref, kept_ref, *rest):
        piece_refs, out_ref = rest[:X], rest[X]
        x, y, core, zh = at_ref[0], at_ref[1], at_ref[2], at_ref[3]
        rows = hidden_ref[...].astype(F32)
        units = depth // (CORES * ZL)
        rows = jnp.concatenate(
            [
                rows[(side * ZL + zl) * units : (side * ZL + zl + 1) * units]
                for zl in range(ZL)
                for side in range(CORES)
            ],
            axis=0,
        )
        lhs = rows.T.astype(BF16)
        kept_rows = kept_ref[...].astype(F32).T
        adds = (y // 2 == core) & (zh == 0)
        left = jnp.where(adds & (lax.rem(y, 2) == 0), 1.0, 0.0)
        right = jnp.where(adds & (lax.rem(y, 2) == 1), 1.0, 0.0)
        for shift in range(X):
            total = jnp.dot(lhs, piece_refs[shift][...], preferred_element_type=F32)
            if shift == 0:
                total = total + jnp.concatenate([kept_rows * left, kept_rows * right], axis=1)
            total = total.astype(BF16)
            start = lax.rem(x - shift + X, X) * cols
            place = pl.ds(pl.multiple_of(start, cols), cols)
            for side in range(CORES):
                for to in range(X * Y):
                    row = side * (tokens // CORES) + to * near
                    out_ref[to, side * near : (side + 1) * near, place] = total[row : row + near]

    return pl.pallas_call(
        kernel,
        out_shape=jax.ShapeDtypeStruct((X * Y, CORES * near, X * cols), BF16),
        in_specs=[smem(), vmem(), vmem()] + [vmem()] * X,
        out_specs=vmem(),
        compiler_params=pltpu.CompilerParams(vmem_limit_bytes=10 * 1024 * 1024),
        name="down",
    )(at, hidden, kept, *pieces)


def sum_and_replicate(parts, count):
    pieces, rows, width = parts.shape

    def kernel(parts_ref, out_ref):
        total = parts_ref[0].astype(F32)
        for piece in range(1, pieces):
            total = total + parts_ref[piece].astype(F32)
        for to in range(count):
            out_ref[to] = total.astype(BF16)

    return pl.pallas_call(
        kernel,
        out_shape=jax.ShapeDtypeStruct((count, rows, width), BF16),
        in_specs=[vmem()],
        out_specs=vmem(),
        compiler_params=pltpu.CompilerParams(vmem_limit_bytes=4 * 1024 * 1024),
        name="sum_and_replicate",
    )(parts)


def carried_and_squares(parts, count):
    pieces, rows, width = parts.shape

    def kernel(parts_ref, out_ref):
        total = parts_ref[0].astype(F32)
        for piece in range(1, pieces):
            total = total + parts_ref[piece].astype(F32)
        square = jnp.sum(total * total, axis=0, keepdims=True)
        high = square.astype(BF16).astype(F32)
        tail = jnp.concatenate(
            [high, square - high, jnp.zeros((EXTRA - 2, width), F32)], axis=0
        ).astype(BF16)
        for to in range(count):
            out_ref[to, :rows, :] = total.astype(BF16)
            out_ref[to, rows:, :] = tail

    return pl.pallas_call(
        kernel,
        out_shape=jax.ShapeDtypeStruct((count, rows + EXTRA, width), BF16),
        in_specs=[vmem()],
        out_specs=vmem(),
        compiler_params=pltpu.CompilerParams(vmem_limit_bytes=4 * 1024 * 1024),
        name="carried_and_squares",
    )(parts)


def activate(parts, d, count):
    pieces, rows, tokens = parts.shape
    units = (rows - EXTRA) // 2

    def kernel(parts_ref, out_ref):
        total = parts_ref[0].astype(F32)
        for piece in range(1, pieces):
            total = total + parts_ref[piece].astype(F32)
        square = total[2 * units : 2 * units + 1] + total[2 * units + 1 : 2 * units + 2]
        scale = lax.rsqrt(square * (1.0 / d) + EPS)
        gate = total[:units] * scale
        up = total[units : 2 * units] * scale
        hidden = (gate / (1.0 + jnp.exp(-gate)) * up).astype(BF16)
        for to in range(count):
            out_ref[to] = hidden

    return pl.pallas_call(
        kernel,
        out_shape=jax.ShapeDtypeStruct((count, units, tokens), BF16),
        in_specs=[vmem()],
        out_specs=vmem(),
        compiler_params=pltpu.CompilerParams(vmem_limit_bytes=4 * 1024 * 1024),
        name="activate",
    )(parts)


def gate_up(spread, pieces, at, done=None):
    blocks, rows, half = spread.shape
    part = rows - EXTRA
    both, depth = pieces[0].shape
    width = half if done is None else CORES * half

    def kernel(at_ref, spread_ref, *rest):
        piece_refs, rest = rest[:Y], rest[Y:]
        if done is not None:
            done_refs, rest = rest[:2], rest[2:]
        out_ref, carried_ref, weights, rhs = rest
        y, core, mine = at_ref[0], at_ref[1], at_ref[2]
        place = slice(None)
        if done is not None:
            own = pl.ds(pl.multiple_of(core * half, half), half)
            place = pl.ds(pl.multiple_of((1 - core) * half, half), half)
            out_ref[:, :, own] = done_refs[0][...]
            carried_ref[:, own] = done_refs[1][...]
        for shift in range(Y):
            to = lax.rem(y - shift + Y, Y)
            weights[pl.ds(pl.multiple_of(to * both, both), both), :] = piece_refs[shift][...]
        square = jnp.zeros((2, half), F32)
        for block in range(blocks):
            rhs[block * part : (block + 1) * part, :] = spread_ref[block, :part, :]
            square = square + spread_ref[block, part : part + 2, :].astype(F32)
        square = square[0:1] + square[1:2]
        high = square.astype(BF16).astype(F32)
        tail = jnp.concatenate(
            [high, square - high, jnp.zeros((EXTRA - 2, half), F32)], axis=0
        ).astype(BF16)
        carried_ref[:, place] = spread_ref[mine, :part, :]
        total = jnp.dot(weights[...], rhs[...], preferred_element_type=F32)
        for to in range(Y):
            out_ref[to, :both, place] = total[to * both : (to + 1) * both].astype(BF16)
            out_ref[to, both:, place] = tail

    extra = () if done is None else tuple(done)
    return pl.pallas_call(
        kernel,
        out_shape=[
            jax.ShapeDtypeStruct((Y, both + EXTRA, width), BF16),
            jax.ShapeDtypeStruct((part, width), BF16),
        ],
        in_specs=[smem(), vmem()] + [vmem()] * (Y + len(extra)),
        out_specs=[vmem(), vmem()],
        scratch_shapes=[
            pltpu.VMEM((Y * both, depth), BF16),
            pltpu.VMEM((depth, half), BF16),
        ],
        compiler_params=pltpu.CompilerParams(vmem_limit_bytes=8 * 1024 * 1024),
        name="gate_up" if done is None else "gate_up_both",
    )(at, spread, *pieces, *extra)


def shards(attention_out, w_out, residual, norm_gain, w_gate, w_up, w_down):
    x_at = lax.axis_index("x")
    zl_at = lax.axis_index("zl")
    core_at = lax.axis_index("core")
    y_at = lax.axis_index("y")
    zh_at = lax.axis_index("zh")
    d = residual.shape[1]
    t_rows = attention_out.shape[0]
    cols = w_out.shape[1]
    units = w_gate.shape[0]
    blocks = X * ZL
    half = t_rows * blocks
    tokens = half * CORES
    part = CORES * cols // Y

    cut = cut_weights(w_gate, w_up, norm_gain, y_at)
    first_piece, third_piece = shift_along(cut[1], "y", 1), shift_along(cut[3], "y", 3)
    by_x = w_down.reshape(X, ZL * CORES * units, cols)
    down_cut = [
        lax.dynamic_index_in_dim(by_x, (x_at + shift) % X, 0, keepdims=False)
        for shift in range(X)
    ]
    w_other = swap_cores(w_out)

    got = exchange(pack_rows(attention_out, residual), ("x", "zl"))
    partial = project(got, w_out, w_other, jnp.stack([y_at, zh_at, core_at]))
    by_y = exchange(partial, "y")
    over_y, first_piece, third_piece, cut, down_cut = lax.optimization_barrier(
        (sum_and_replicate(by_y, ZH), first_piece, third_piece, cut, down_cut)
    )
    second_piece = shift_along(cut[2], "y", 2)
    down_pieces = [down_cut[0]] + [
        shift_along(down_cut[shift], "x", shift) if shift != 2 else None for shift in range(1, X)
    ]
    by_zh = exchange(over_y, "zh")
    by_zh, second_piece, down_pieces[1], down_pieces[3], down_cut = lax.optimization_barrier(
        (by_zh, second_piece, down_pieces[1], down_pieces[3], down_cut)
    )
    down_pieces[2] = shift_along(down_cut[2], "x", 2)
    pieces = [cut[0], first_piece, second_piece, third_piece]
    spread, down_pieces[2] = lax.optimization_barrier(
        (exchange(carried_and_squares(by_zh, ZL), "zl"), down_pieces[2])
    )
    spread = exchange(replicate(spread, X), "x")
    spread = spread.reshape(blocks, part + EXTRA, half)
    other = swap_cores(spread)
    at = jnp.stack([y_at, core_at, x_at * ZL + zl_at])
    outs, kept = gate_up(other, pieces, at, gate_up(spread, pieces, at))
    hidden = exchange(activate(exchange(outs, "y"), d, ZL), "zl")
    hidden = lax.all_gather(hidden, "core", axis=0, tiled=False)
    by_owner = down(
        hidden.reshape(CORES * ZL * units, tokens),
        down_pieces,
        kept,
        jnp.stack([x_at, y_at, core_at, zh_at]),
    )
    near = sum_and_replicate(exchange(by_owner, ("x", "y")), 1)
    near = near.reshape(CORES * ZL * ZH, X * cols // 128, 128)
    final = exchange(near, ("core", "zl", "zh"))
    final = final.reshape(CORES, ZL, ZH, X, cols).astype(F32)
    mixed = jnp.sum(final, axis=2)
    mixed = jnp.transpose(mixed, (2, 1, 0, 3)).reshape(1, d)
    return mixed.astype(BF16)


def solution(mesh):
    view = Mesh(
        mesh.devices.reshape(X, ZL, CORES, Y, ZH), ("x", "zl", "core", "y", "zh")
    )
    ctx = ("x", "zl", "core")
    tp = ("y", "zh")
    in_specs = (
        P(ctx, tp),
        P(tp, ctx),
        P(ctx + tp, None),
        P(),
        P(ctx + tp, None),
        P(ctx + tp, None),
        P(None, tp, ctx),
    )
    return jax.shard_map(
        shards, mesh=view, in_specs=in_specs, out_specs=P(ctx + tp, None), check_vma=False
    )
```

```python
import jax
import jax.numpy as jnp
from jax import lax
from jax.experimental import pallas as pl
from jax.experimental.pallas import tpu as pltpu
from jax.sharding import Mesh, PartitionSpec as P

F32 = jnp.float32
BF16 = jnp.bfloat16
EPS = 1e-05
X, ZL, Y, ZH = 4, 4, 4, 4
CORES = 2
EXTRA = 8


def exchange(value, axes):
    return lax.all_to_all(value, axes, 0, 0, tiled=True)


def replicate(value, count):
    return lax.optimization_barrier(jnp.broadcast_to(value[None], (count,) + value.shape))


def swap_cores(value):
    return lax.ppermute(value, "core", [(0, 1), (1, 0)])


def shift_along(value, axis, shift):
    return lax.ppermute(value, axis, [(i, (i + shift) % 4) for i in range(4)])


def vmem():
    return pl.BlockSpec(memory_space=pltpu.VMEM)


def smem():
    return pl.BlockSpec(memory_space=pltpu.SMEM)


def pack_rows(attention_out, residual):
    t_rows, heads = attention_out.shape
    wide = residual.shape[1] // (X * ZL)
    rows = 24

    def kernel(att_ref, res_ref, sent_ref):
        for to in range(X * ZL):
            sent_ref[to, :t_rows, :] = att_ref[...]
            sent_ref[to, t_rows:, :] = jnp.zeros((rows - t_rows, heads), BF16)
            sent_ref[to, t_rows : t_rows + 1, :] = res_ref[:, to * wide : (to + 1) * wide]

    return pl.pallas_call(
        kernel,
        out_shape=jax.ShapeDtypeStruct((X * ZL, rows, heads), BF16),
        in_specs=[vmem(), vmem()],
        out_specs=vmem(),
        compiler_params=pltpu.CompilerParams(vmem_limit_bytes=56 * 1024 * 1024),
        name="pack_rows",
    )(attention_out, residual)


def cut_weights(w_gate, w_up, norm_gain, y_at):
    units, d = w_gate.shape
    blocks = X * ZL
    wide = d // blocks
    part = wide // Y

    def kernel(at_ref, gate_ref, up_ref, gain_ref, *piece_refs):
        for shift in range(Y):
            to = lax.rem(at_ref[0] + shift, Y)
            for block in range(blocks):
                place = pl.ds(pl.multiple_of(block * wide + to * part, part), part)
                gain = gain_ref[:, place]
                both = jnp.concatenate(
                    [gate_ref[:, place].astype(F32) * gain, up_ref[:, place].astype(F32) * gain],
                    axis=0,
                )
                piece_refs[shift][:, block * part : (block + 1) * part] = both.astype(BF16)

    return pl.pallas_call(
        kernel,
        out_shape=[jax.ShapeDtypeStruct((2 * units, blocks * part), BF16)] * Y,
        in_specs=[smem(), vmem(), vmem(), vmem()],
        out_specs=[vmem()] * Y,
        compiler_params=pltpu.CompilerParams(vmem_limit_bytes=12 * 1024 * 1024),
        name="cut_weights",
    )(y_at.reshape(1), w_gate, w_up, norm_gain.reshape(1, d))


def project(got, w_out, w_other, at):
    blocks, _, heads = got.shape
    cols = w_out.shape[1]
    t_rows = Y * ZH
    half = blocks * t_rows
    part = CORES * cols // Y

    def kernel(at_ref, got_ref, own_ref, other_ref, out_ref, att, res):
        y, zh, core = at_ref[0], at_ref[1], at_ref[2]
        for x in range(X):
            for zl in range(ZL):
                block = x * ZL + zl
                for row in range(Y):
                    to = ((x * Y + row) * ZL + zl) * ZH
                    att[to : to + ZH, :] = got_ref[block, row * ZH : (row + 1) * ZH, :]
                res[block : block + 1, :] = got_ref[block, t_rows : t_rows + 1, :]
        token = lax.broadcasted_iota(jnp.int32, (half, blocks), 0)
        source = lax.broadcasted_iota(jnp.int32, (half, blocks), 1)
        place = ((source // ZL) * Y + y) * t_rows + lax.rem(source, ZL) * ZH + zh
        pick = jnp.where(token == place, 1.0, 0.0).astype(BF16)
        for turn, ref in enumerate((own_ref, other_ref)):
            side = core if turn == 0 else 1 - core
            columns = pl.ds(pl.multiple_of(side * cols, cols), cols)
            total = jnp.dot(att[...], ref[...], preferred_element_type=F32) + jnp.dot(
                pick, res[:, columns], preferred_element_type=F32
            )
            total = total.T.astype(BF16)
            for piece in range(cols // part):
                out_ref[side * (cols // part) + piece] = total[piece * part : (piece + 1) * part]

    return pl.pallas_call(
        kernel,
        out_shape=jax.ShapeDtypeStruct((Y, part, half), BF16),
        in_specs=[smem(), vmem(), vmem(), vmem()],
        out_specs=vmem(),
        scratch_shapes=[pltpu.VMEM((half, heads), BF16), pltpu.VMEM((blocks, heads), BF16)],
        compiler_params=pltpu.CompilerParams(vmem_limit_bytes=6 * 1024 * 1024),
        name="project",
    )(at, got, w_out, w_other)


def down(hidden, pieces, kept, at):
    depth, tokens = hidden.shape
    cols = pieces[0].shape[1]
    part = kept.shape[0]
    near = tokens // (X * Y * CORES)

    def kernel(at_ref, hidden_ref, kept_ref, *rest):
        piece_refs, out_ref = rest[:X], rest[X]
        x, y, core, zh = at_ref[0], at_ref[1], at_ref[2], at_ref[3]
        rows = hidden_ref[...].astype(F32)
        units = depth // (CORES * ZL)
        rows = jnp.concatenate(
            [
                rows[(side * ZL + zl) * units : (side * ZL + zl + 1) * units]
                for zl in range(ZL)
                for side in range(CORES)
            ],
            axis=0,
        )
        lhs = rows.T.astype(BF16)
        kept_rows = kept_ref[...].astype(F32).T
        adds = (y // 2 == core) & (zh == 0)
        left = jnp.where(adds & (lax.rem(y, 2) == 0), 1.0, 0.0)
        right = jnp.where(adds & (lax.rem(y, 2) == 1), 1.0, 0.0)
        for shift in range(X):
            total = jnp.dot(lhs, piece_refs[shift][...], preferred_element_type=F32)
            if shift == 0:
                total = total + jnp.concatenate([kept_rows * left, kept_rows * right], axis=1)
            total = total.astype(BF16)
            start = lax.rem(x - shift + X, X) * cols
            place = pl.ds(pl.multiple_of(start, cols), cols)
            for side in range(CORES):
                for to in range(X * Y):
                    row = side * (tokens // CORES) + to * near
                    out_ref[to, side * near : (side + 1) * near, place] = total[row : row + near]

    return pl.pallas_call(
        kernel,
        out_shape=jax.ShapeDtypeStruct((X * Y, CORES * near, X * cols), BF16),
        in_specs=[smem(), vmem(), vmem()] + [vmem()] * X,
        out_specs=vmem(),
        compiler_params=pltpu.CompilerParams(vmem_limit_bytes=10 * 1024 * 1024),
        name="down",
    )(at, hidden, kept, *pieces)


def sum_to_row(parts, d):
    _, rows, lanes = parts.shape
    per_x = rows // X

    def kernel(parts_ref, out_ref):
        for zl in range(ZL):
            for core in range(CORES):
                first = (core * ZL + zl) * ZH
                total = parts_ref[first].astype(F32)
                for zh in range(1, ZH):
                    total = total + parts_ref[first + zh].astype(F32)
                for row in range(rows):
                    x, piece = row // per_x, row % per_x
                    at = (((x * ZL + zl) * CORES + core) * per_x + piece) * lanes
                    out_ref[:, at : at + lanes] = total[row : row + 1].astype(BF16)

    return pl.pallas_call(
        kernel,
        out_shape=jax.ShapeDtypeStruct((1, d), BF16),
        in_specs=[vmem()],
        out_specs=vmem(),
        compiler_params=pltpu.CompilerParams(vmem_limit_bytes=4 * 1024 * 1024),
        name="sum_to_row",
    )(parts)


def sum_and_replicate(parts, count):
    pieces, rows, width = parts.shape

    def kernel(parts_ref, out_ref):
        total = parts_ref[0].astype(F32)
        for piece in range(1, pieces):
            total = total + parts_ref[piece].astype(F32)
        for to in range(count):
            out_ref[to] = total.astype(BF16)

    return pl.pallas_call(
        kernel,
        out_shape=jax.ShapeDtypeStruct((count, rows, width), BF16),
        in_specs=[vmem()],
        out_specs=vmem(),
        compiler_params=pltpu.CompilerParams(vmem_limit_bytes=4 * 1024 * 1024),
        name="sum_and_replicate",
    )(parts)


def carried_and_squares(parts, count):
    pieces, rows, width = parts.shape

    def kernel(parts_ref, out_ref):
        total = parts_ref[0].astype(F32)
        for piece in range(1, pieces):
            total = total + parts_ref[piece].astype(F32)
        square = jnp.sum(total * total, axis=0, keepdims=True)
        high = square.astype(BF16).astype(F32)
        tail = jnp.concatenate(
            [high, square - high, jnp.zeros((EXTRA - 2, width), F32)], axis=0
        ).astype(BF16)
        for to in range(count):
            out_ref[to, :rows, :] = total.astype(BF16)
            out_ref[to, rows:, :] = tail

    return pl.pallas_call(
        kernel,
        out_shape=jax.ShapeDtypeStruct((count, rows + EXTRA, width), BF16),
        in_specs=[vmem()],
        out_specs=vmem(),
        compiler_params=pltpu.CompilerParams(vmem_limit_bytes=4 * 1024 * 1024),
        name="carried_and_squares",
    )(parts)


def activate(parts, d, count):
    pieces, rows, tokens = parts.shape
    units = (rows - EXTRA) // 2

    def kernel(parts_ref, out_ref):
        total = parts_ref[0].astype(F32)
        for piece in range(1, pieces):
            total = total + parts_ref[piece].astype(F32)
        square = total[2 * units : 2 * units + 1] + total[2 * units + 1 : 2 * units + 2]
        scale = lax.rsqrt(square * (1.0 / d) + EPS)
        gate = total[:units] * scale
        up = total[units : 2 * units] * scale
        hidden = (gate / (1.0 + jnp.exp(-gate)) * up).astype(BF16)
        for to in range(count):
            out_ref[to] = hidden

    return pl.pallas_call(
        kernel,
        out_shape=jax.ShapeDtypeStruct((count, units, tokens), BF16),
        in_specs=[vmem()],
        out_specs=vmem(),
        compiler_params=pltpu.CompilerParams(vmem_limit_bytes=4 * 1024 * 1024),
        name="activate",
    )(parts)


def gate_up(spread, pieces, at, done=None):
    blocks, rows, half = spread.shape
    part = rows - EXTRA
    both, depth = pieces[0].shape
    width = half if done is None else CORES * half

    def kernel(at_ref, spread_ref, *rest):
        piece_refs, rest = rest[:Y], rest[Y:]
        if done is not None:
            done_refs, rest = rest[:2], rest[2:]
        out_ref, carried_ref, weights, rhs = rest
        y, core, mine = at_ref[0], at_ref[1], at_ref[2]
        place = slice(None)
        if done is not None:
            own = pl.ds(pl.multiple_of(core * half, half), half)
            place = pl.ds(pl.multiple_of((1 - core) * half, half), half)
            out_ref[:, :, own] = done_refs[0][...]
            carried_ref[:, own] = done_refs[1][...]
        for shift in range(Y):
            to = lax.rem(y - shift + Y, Y)
            weights[pl.ds(pl.multiple_of(to * both, both), both), :] = piece_refs[shift][...]
        square = jnp.zeros((2, half), F32)
        for block in range(blocks):
            rhs[block * part : (block + 1) * part, :] = spread_ref[block, :part, :]
            square = square + spread_ref[block, part : part + 2, :].astype(F32)
        square = square[0:1] + square[1:2]
        high = square.astype(BF16).astype(F32)
        tail = jnp.concatenate(
            [high, square - high, jnp.zeros((EXTRA - 2, half), F32)], axis=0
        ).astype(BF16)
        carried_ref[:, place] = spread_ref[mine, :part, :]
        total = jnp.dot(weights[...], rhs[...], preferred_element_type=F32)
        for to in range(Y):
            out_ref[to, :both, place] = total[to * both : (to + 1) * both].astype(BF16)
            out_ref[to, both:, place] = tail

    extra = () if done is None else tuple(done)
    return pl.pallas_call(
        kernel,
        out_shape=[
            jax.ShapeDtypeStruct((Y, both + EXTRA, width), BF16),
            jax.ShapeDtypeStruct((part, width), BF16),
        ],
        in_specs=[smem(), vmem()] + [vmem()] * (Y + len(extra)),
        out_specs=[vmem(), vmem()],
        scratch_shapes=[
            pltpu.VMEM((Y * both, depth), BF16),
            pltpu.VMEM((depth, half), BF16),
        ],
        compiler_params=pltpu.CompilerParams(vmem_limit_bytes=8 * 1024 * 1024),
        name="gate_up" if done is None else "gate_up_both",
    )(at, spread, *pieces, *extra)


def shards(attention_out, w_out, residual, norm_gain, w_gate, w_up, w_down):
    x_at = lax.axis_index("x")
    zl_at = lax.axis_index("zl")
    core_at = lax.axis_index("core")
    y_at = lax.axis_index("y")
    zh_at = lax.axis_index("zh")
    d = residual.shape[1]
    t_rows = attention_out.shape[0]
    cols = w_out.shape[1]
    units = w_gate.shape[0]
    blocks = X * ZL
    half = t_rows * blocks
    tokens = half * CORES
    part = CORES * cols // Y

    cut = cut_weights(w_gate, w_up, norm_gain, y_at)
    first_piece, third_piece = shift_along(cut[1], "y", 1), shift_along(cut[3], "y", 3)
    by_x = w_down.reshape(X, ZL * CORES * units, cols)
    down_cut = [
        lax.dynamic_index_in_dim(by_x, (x_at + shift) % X, 0, keepdims=False)
        for shift in range(X)
    ]
    w_other = swap_cores(w_out)

    got = exchange(pack_rows(attention_out, residual), ("x", "zl"))
    partial = project(got, w_out, w_other, jnp.stack([y_at, zh_at, core_at]))
    by_y = exchange(partial, "y")
    over_y, first_piece, third_piece, cut, down_cut = lax.optimization_barrier(
        (sum_and_replicate(by_y, ZH), first_piece, third_piece, cut, down_cut)
    )
    second_piece = shift_along(cut[2], "y", 2)
    down_pieces = [down_cut[0]] + [
        shift_along(down_cut[shift], "x", shift) if shift != 2 else None for shift in range(1, X)
    ]
    by_zh = exchange(over_y, "zh")
    by_zh, second_piece, down_pieces[1], down_pieces[3], down_cut = lax.optimization_barrier(
        (by_zh, second_piece, down_pieces[1], down_pieces[3], down_cut)
    )
    down_pieces[2] = shift_along(down_cut[2], "x", 2)
    pieces = [cut[0], first_piece, second_piece, third_piece]
    spread, down_pieces[2] = lax.optimization_barrier(
        (exchange(carried_and_squares(by_zh, ZL), "zl"), down_pieces[2])
    )
    spread = exchange(replicate(spread, X), "x")
    spread = spread.reshape(blocks, part + EXTRA, half)
    other = swap_cores(spread)
    at = jnp.stack([y_at, core_at, x_at * ZL + zl_at])
    outs, kept = gate_up(other, pieces, at, gate_up(spread, pieces, at))
    hidden = exchange(activate(exchange(outs, "y"), d, ZL), "zl")
    hidden = lax.all_gather(hidden, "core", axis=0, tiled=False)
    by_owner = down(
        hidden.reshape(CORES * ZL * units, tokens),
        down_pieces,
        kept,
        jnp.stack([x_at, y_at, core_at, zh_at]),
    )
    near = sum_and_replicate(exchange(by_owner, ("x", "y")), 1)
    near = near.reshape(CORES * ZL * ZH, X * cols // 128, 128)
    final = exchange(near, ("core", "zl", "zh"))
    return sum_to_row(final, d)


def solution(mesh):
    view = Mesh(
        mesh.devices.reshape(X, ZL, CORES, Y, ZH), ("x", "zl", "core", "y", "zh")
    )
    ctx = ("x", "zl", "core")
    tp = ("y", "zh")
    in_specs = (
        P(ctx, tp),
        P(tp, ctx),
        P(ctx + tp, None),
        P(),
        P(ctx + tp, None),
        P(ctx + tp, None),
        P(None, tp, ctx),
    )
    return jax.shard_map(
        shards, mesh=view, in_specs=in_specs, out_specs=P(ctx + tp, None), check_vma=False
    )
```

```python
import jax
import jax.numpy as jnp
from jax import lax
from jax.experimental import pallas as pl
from jax.experimental.pallas import tpu as pltpu
from jax.sharding import Mesh, PartitionSpec as P

F32 = jnp.float32
BF16 = jnp.bfloat16
EPS = 1e-05
X, ZL, Y, ZH = 4, 4, 4, 4
CORES = 2
EXTRA = 8


def exchange(value, axes):
    return lax.all_to_all(value, axes, 0, 0, tiled=True)


def replicate(value, count):
    return lax.optimization_barrier(jnp.broadcast_to(value[None], (count,) + value.shape))


def swap_cores(value):
    return lax.ppermute(value, "core", [(0, 1), (1, 0)])


def shift_along(value, axis, shift):
    return lax.ppermute(value, axis, [(i, (i + shift) % 4) for i in range(4)])


def vmem():
    return pl.BlockSpec(memory_space=pltpu.VMEM)


def smem():
    return pl.BlockSpec(memory_space=pltpu.SMEM)


def pack_rows(attention_out, residual):
    t_rows, heads = attention_out.shape
    wide = residual.shape[1] // (X * ZL)
    rows = 24

    def kernel(att_ref, res_ref, sent_ref):
        for to in range(X * ZL):
            sent_ref[to, :t_rows, :] = att_ref[...]
            sent_ref[to, t_rows:, :] = jnp.zeros((rows - t_rows, heads), BF16)
            sent_ref[to, t_rows : t_rows + 1, :] = res_ref[:, to * wide : (to + 1) * wide]

    return pl.pallas_call(
        kernel,
        out_shape=jax.ShapeDtypeStruct((X * ZL, rows, heads), BF16),
        in_specs=[vmem(), vmem()],
        out_specs=vmem(),
        compiler_params=pltpu.CompilerParams(vmem_limit_bytes=56 * 1024 * 1024),
        name="pack_rows",
    )(attention_out, residual)


def cut_weights(w_gate, w_up, norm_gain, y_at):
    units, d = w_gate.shape
    blocks = X * ZL
    wide = d // blocks
    part = wide // Y

    def kernel(at_ref, gate_ref, up_ref, gain_ref, *piece_refs):
        for shift in range(Y):
            to = lax.rem(at_ref[0] + shift, Y)
            for block in range(blocks):
                place = pl.ds(pl.multiple_of(block * wide + to * part, part), part)
                gain = gain_ref[:, place]
                both = jnp.concatenate(
                    [gate_ref[:, place].astype(F32) * gain, up_ref[:, place].astype(F32) * gain],
                    axis=0,
                )
                piece_refs[shift][:, block * part : (block + 1) * part] = both.astype(BF16)

    return pl.pallas_call(
        kernel,
        out_shape=[jax.ShapeDtypeStruct((2 * units, blocks * part), BF16)] * Y,
        in_specs=[smem(), vmem(), vmem(), vmem()],
        out_specs=[vmem()] * Y,
        compiler_params=pltpu.CompilerParams(vmem_limit_bytes=12 * 1024 * 1024),
        name="cut_weights",
    )(y_at.reshape(1), w_gate, w_up, norm_gain.reshape(1, d))


def project(got, w_out, w_other, at):
    blocks, _, heads = got.shape
    cols = w_out.shape[1]
    t_rows = Y * ZH
    half = blocks * t_rows
    part = CORES * cols // Y

    def kernel(at_ref, got_ref, own_ref, other_ref, out_ref, att, res):
        y, zh, core = at_ref[0], at_ref[1], at_ref[2]
        for x in range(X):
            for zl in range(ZL):
                block = x * ZL + zl
                for row in range(Y):
                    to = ((x * Y + row) * ZL + zl) * ZH
                    att[to : to + ZH, :] = got_ref[block, row * ZH : (row + 1) * ZH, :]
                res[block : block + 1, :] = got_ref[block, t_rows : t_rows + 1, :]
        token = lax.broadcasted_iota(jnp.int32, (half, blocks), 0)
        source = lax.broadcasted_iota(jnp.int32, (half, blocks), 1)
        place = ((source // ZL) * Y + y) * t_rows + lax.rem(source, ZL) * ZH + zh
        pick = jnp.where(token == place, 1.0, 0.0).astype(BF16)
        for turn, ref in enumerate((own_ref, other_ref)):
            side = core if turn == 0 else 1 - core
            columns = pl.ds(pl.multiple_of(side * cols, cols), cols)
            total = jnp.dot(att[...], ref[...], preferred_element_type=F32) + jnp.dot(
                pick, res[:, columns], preferred_element_type=F32
            )
            total = total.T.astype(BF16)
            for piece in range(cols // part):
                out_ref[side * (cols // part) + piece] = total[piece * part : (piece + 1) * part]

    return pl.pallas_call(
        kernel,
        out_shape=jax.ShapeDtypeStruct((Y, part, half), BF16),
        in_specs=[smem(), vmem(), vmem(), vmem()],
        out_specs=vmem(),
        scratch_shapes=[pltpu.VMEM((half, heads), BF16), pltpu.VMEM((blocks, heads), BF16)],
        compiler_params=pltpu.CompilerParams(vmem_limit_bytes=6 * 1024 * 1024),
        name="project",
    )(at, got, w_out, w_other)


def down(hidden, pieces, kept, at):
    depth, tokens = hidden.shape
    cols = pieces[0].shape[1]
    part = kept.shape[0]
    near = tokens // (X * Y * CORES)

    def kernel(at_ref, hidden_ref, kept_ref, *rest):
        piece_refs, out_ref = rest[:X], rest[X]
        x, y, core, zh = at_ref[0], at_ref[1], at_ref[2], at_ref[3]
        rows = hidden_ref[...].astype(F32)
        units = depth // (CORES * ZL)
        rows = jnp.concatenate(
            [
                rows[(side * ZL + zl) * units : (side * ZL + zl + 1) * units]
                for zl in range(ZL)
                for side in range(CORES)
            ],
            axis=0,
        )
        lhs = rows.T.astype(BF16)
        kept_rows = kept_ref[...].astype(F32).T
        adds = (y // 2 == core) & (zh == 0)
        left = jnp.where(adds & (lax.rem(y, 2) == 0), 1.0, 0.0)
        right = jnp.where(adds & (lax.rem(y, 2) == 1), 1.0, 0.0)
        for shift in range(X):
            total = jnp.dot(lhs, piece_refs[shift][...], preferred_element_type=F32)
            if shift == 0:
                total = total + jnp.concatenate([kept_rows * left, kept_rows * right], axis=1)
            total = total.astype(BF16)
            start = lax.rem(x - shift + X, X) * cols
            place = pl.ds(pl.multiple_of(start, cols), cols)
            for side in range(CORES):
                for to in range(X * Y):
                    row = side * (tokens // CORES) + to * near
                    out_ref[to, side * near : (side + 1) * near, place] = total[row : row + near]

    return pl.pallas_call(
        kernel,
        out_shape=jax.ShapeDtypeStruct((X * Y, CORES * near, X * cols), BF16),
        in_specs=[smem(), vmem(), vmem()] + [vmem()] * X,
        out_specs=vmem(),
        compiler_params=pltpu.CompilerParams(vmem_limit_bytes=10 * 1024 * 1024),
        name="down",
    )(at, hidden, kept, *pieces)


def sum_by_token(parts):
    pieces, rows, width = parts.shape

    def kernel(parts_ref, out_ref):
        total = parts_ref[0].astype(F32)
        for piece in range(1, pieces):
            total = total + parts_ref[piece].astype(F32)
        out_ref[...] = total.reshape(rows, width // 128, 128).astype(BF16)

    return pl.pallas_call(
        kernel,
        out_shape=jax.ShapeDtypeStruct((rows, width // 128, 128), BF16),
        in_specs=[vmem()],
        out_specs=vmem(),
        compiler_params=pltpu.CompilerParams(vmem_limit_bytes=4 * 1024 * 1024),
        name="sum_by_token",
    )(parts)


def sum_to_row(parts, d):
    _, rows, lanes = parts.shape
    per_x = rows // X

    def kernel(parts_ref, out_ref):
        for zl in range(ZL):
            for core in range(CORES):
                first = (core * ZL + zl) * ZH
                total = parts_ref[first].astype(F32)
                for zh in range(1, ZH):
                    total = total + parts_ref[first + zh].astype(F32)
                for row in range(rows):
                    x, piece = row // per_x, row % per_x
                    at = (((x * ZL + zl) * CORES + core) * per_x + piece) * lanes
                    out_ref[:, at : at + lanes] = total[row : row + 1].astype(BF16)

    return pl.pallas_call(
        kernel,
        out_shape=jax.ShapeDtypeStruct((1, d), BF16),
        in_specs=[vmem()],
        out_specs=vmem(),
        compiler_params=pltpu.CompilerParams(vmem_limit_bytes=4 * 1024 * 1024),
        name="sum_to_row",
    )(parts)


def sum_and_replicate(parts, count):
    pieces, rows, width = parts.shape

    def kernel(parts_ref, out_ref):
        total = parts_ref[0].astype(F32)
        for piece in range(1, pieces):
            total = total + parts_ref[piece].astype(F32)
        for to in range(count):
            out_ref[to] = total.astype(BF16)

    return pl.pallas_call(
        kernel,
        out_shape=jax.ShapeDtypeStruct((count, rows, width), BF16),
        in_specs=[vmem()],
        out_specs=vmem(),
        compiler_params=pltpu.CompilerParams(vmem_limit_bytes=4 * 1024 * 1024),
        name="sum_and_replicate",
    )(parts)


def carried_and_squares(parts, count):
    pieces, rows, width = parts.shape

    def kernel(parts_ref, out_ref):
        total = parts_ref[0].astype(F32)
        for piece in range(1, pieces):
            total = total + parts_ref[piece].astype(F32)
        square = jnp.sum(total * total, axis=0, keepdims=True)
        high = square.astype(BF16).astype(F32)
        tail = jnp.concatenate(
            [high, square - high, jnp.zeros((EXTRA - 2, width), F32)], axis=0
        ).astype(BF16)
        for to in range(count):
            out_ref[to, :rows, :] = total.astype(BF16)
            out_ref[to, rows:, :] = tail

    return pl.pallas_call(
        kernel,
        out_shape=jax.ShapeDtypeStruct((count, rows + EXTRA, width), BF16),
        in_specs=[vmem()],
        out_specs=vmem(),
        compiler_params=pltpu.CompilerParams(vmem_limit_bytes=4 * 1024 * 1024),
        name="carried_and_squares",
    )(parts)


def activate(parts, d, count):
    pieces, rows, tokens = parts.shape
    units = (rows - EXTRA) // 2

    def kernel(parts_ref, out_ref):
        total = parts_ref[0].astype(F32)
        for piece in range(1, pieces):
            total = total + parts_ref[piece].astype(F32)
        square = total[2 * units : 2 * units + 1] + total[2 * units + 1 : 2 * units + 2]
        scale = lax.rsqrt(square * (1.0 / d) + EPS)
        gate = total[:units] * scale
        up = total[units : 2 * units] * scale
        hidden = (gate / (1.0 + jnp.exp(-gate)) * up).astype(BF16)
        for to in range(count):
            out_ref[to] = hidden

    return pl.pallas_call(
        kernel,
        out_shape=jax.ShapeDtypeStruct((count, units, tokens), BF16),
        in_specs=[vmem()],
        out_specs=vmem(),
        compiler_params=pltpu.CompilerParams(vmem_limit_bytes=4 * 1024 * 1024),
        name="activate",
    )(parts)


def gate_up(spread, pieces, at, done=None):
    blocks, rows, half = spread.shape
    part = rows - EXTRA
    both, depth = pieces[0].shape
    width = half if done is None else CORES * half

    def kernel(at_ref, spread_ref, *rest):
        piece_refs, rest = rest[:Y], rest[Y:]
        if done is not None:
            done_refs, rest = rest[:2], rest[2:]
        out_ref, carried_ref, weights, rhs = rest
        y, core, mine = at_ref[0], at_ref[1], at_ref[2]
        place = slice(None)
        if done is not None:
            own = pl.ds(pl.multiple_of(core * half, half), half)
            place = pl.ds(pl.multiple_of((1 - core) * half, half), half)
            out_ref[:, :, own] = done_refs[0][...]
            carried_ref[:, own] = done_refs[1][...]
        for shift in range(Y):
            to = lax.rem(y - shift + Y, Y)
            weights[pl.ds(pl.multiple_of(to * both, both), both), :] = piece_refs[shift][...]
        square = jnp.zeros((2, half), F32)
        for block in range(blocks):
            rhs[block * part : (block + 1) * part, :] = spread_ref[block, :part, :]
            square = square + spread_ref[block, part : part + 2, :].astype(F32)
        square = square[0:1] + square[1:2]
        high = square.astype(BF16).astype(F32)
        tail = jnp.concatenate(
            [high, square - high, jnp.zeros((EXTRA - 2, half), F32)], axis=0
        ).astype(BF16)
        carried_ref[:, place] = spread_ref[mine, :part, :]
        total = jnp.dot(weights[...], rhs[...], preferred_element_type=F32)
        for to in range(Y):
            out_ref[to, :both, place] = total[to * both : (to + 1) * both].astype(BF16)
            out_ref[to, both:, place] = tail

    extra = () if done is None else tuple(done)
    return pl.pallas_call(
        kernel,
        out_shape=[
            jax.ShapeDtypeStruct((Y, both + EXTRA, width), BF16),
            jax.ShapeDtypeStruct((part, width), BF16),
        ],
        in_specs=[smem(), vmem()] + [vmem()] * (Y + len(extra)),
        out_specs=[vmem(), vmem()],
        scratch_shapes=[
            pltpu.VMEM((Y * both, depth), BF16),
            pltpu.VMEM((depth, half), BF16),
        ],
        compiler_params=pltpu.CompilerParams(vmem_limit_bytes=8 * 1024 * 1024),
        name="gate_up" if done is None else "gate_up_both",
    )(at, spread, *pieces, *extra)


def shards(attention_out, w_out, residual, norm_gain, w_gate, w_up, w_down):
    x_at = lax.axis_index("x")
    zl_at = lax.axis_index("zl")
    core_at = lax.axis_index("core")
    y_at = lax.axis_index("y")
    zh_at = lax.axis_index("zh")
    d = residual.shape[1]
    t_rows = attention_out.shape[0]
    cols = w_out.shape[1]
    units = w_gate.shape[0]
    blocks = X * ZL
    half = t_rows * blocks
    tokens = half * CORES
    part = CORES * cols // Y

    cut = cut_weights(w_gate, w_up, norm_gain, y_at)
    first_piece, third_piece = shift_along(cut[1], "y", 1), shift_along(cut[3], "y", 3)
    by_x = w_down.reshape(X, ZL * CORES * units, cols)
    down_cut = [
        lax.dynamic_index_in_dim(by_x, (x_at + shift) % X, 0, keepdims=False)
        for shift in range(X)
    ]
    w_other = swap_cores(w_out)

    got = exchange(pack_rows(attention_out, residual), ("x", "zl"))
    partial = project(got, w_out, w_other, jnp.stack([y_at, zh_at, core_at]))
    by_y = exchange(partial, "y")
    over_y, first_piece, third_piece, cut, down_cut = lax.optimization_barrier(
        (sum_and_replicate(by_y, ZH), first_piece, third_piece, cut, down_cut)
    )
    second_piece = shift_along(cut[2], "y", 2)
    down_pieces = [down_cut[0]] + [
        shift_along(down_cut[shift], "x", shift) if shift != 2 else None for shift in range(1, X)
    ]
    by_zh = exchange(over_y, "zh")
    by_zh, second_piece, down_pieces[1], down_pieces[3], down_cut = lax.optimization_barrier(
        (by_zh, second_piece, down_pieces[1], down_pieces[3], down_cut)
    )
    down_pieces[2] = shift_along(down_cut[2], "x", 2)
    pieces = [cut[0], first_piece, second_piece, third_piece]
    spread, down_pieces[2] = lax.optimization_barrier(
        (exchange(carried_and_squares(by_zh, ZL), "zl"), down_pieces[2])
    )
    spread = exchange(replicate(spread, X), "x")
    spread = spread.reshape(blocks, part + EXTRA, half)
    other = swap_cores(spread)
    at = jnp.stack([y_at, core_at, x_at * ZL + zl_at])
    outs, kept = gate_up(other, pieces, at, gate_up(spread, pieces, at))
    hidden = exchange(activate(exchange(outs, "y"), d, ZL), "zl")
    hidden = lax.all_gather(hidden, "core", axis=0, tiled=False)
    by_owner = down(
        hidden.reshape(CORES * ZL * units, tokens),
        down_pieces,
        kept,
        jnp.stack([x_at, y_at, core_at, zh_at]),
    )
    near = sum_by_token(exchange(by_owner, ("x", "y")))
    final = exchange(near, ("core", "zl", "zh"))
    return sum_to_row(final, d)


def solution(mesh):
    view = Mesh(
        mesh.devices.reshape(X, ZL, CORES, Y, ZH), ("x", "zl", "core", "y", "zh")
    )
    ctx = ("x", "zl", "core")
    tp = ("y", "zh")
    in_specs = (
        P(ctx, tp),
        P(tp, ctx),
        P(ctx + tp, None),
        P(),
        P(ctx + tp, None),
        P(ctx + tp, None),
        P(None, tp, ctx),
    )
    return jax.shard_map(
        shards, mesh=view, in_specs=in_specs, out_specs=P(ctx + tp, None), check_vma=False
    )
```
